32 devices in a mesh: lon: 8 (over y, x, core), spec: 4 (over z).
Axes of the slice: x: 2, y: 2, z: 4, core: 2. Of those that a mesh axis runs over, the one named last changes fastest.
Arguments:
- lam_final: float32 [1296, 64, 1024], P('spec', None, 'lon'), may hold values from -6 to 6
- stored_source: bfloat16 [2, 1296, 64, 1024], P(None, 'spec', None, 'lon'), may hold values from 0.19921875 to 1.1953125
- mixing: bfloat16 [1296, 1296], replicated, may hold values from -0.15625 to 0.15625
- drift_x: float32 [1296], replicated, may hold values from -0.45 to 0.45
- drift_y: float32 [1296], replicated, may hold values from -0.45 to 0.45
- ocean_mask: int32 [64, 1024], P(None, 'lon'), may hold values 0 or 1
- misfit: float32 [2, 64, 1024], P(None, None, 'lon'), may hold values from -6 to 6
- obs_mask: int32 [2, 64, 1024], P(None, None, 'lon'), may hold values 0 or 1
Outputs:
- lam_start: float32 [1296, 64, 1024], P('spec', None, 'lon')
The draws below stay inside these ranges and needn't reach their ends.
All inputs are finite; a program needn't handle non-finite values. No bound on the sum of `ocean_mask` or of `obs_mask` on one device may be relied on, other than what follows from the above.
Results may differ from the reference program's by a relative error of at most 0.0028.
Values may be sent and summed in bfloat16 or wider, within the bound.
A program may use at most 192 MiB of HBM per device.

```python
import jax
import jax.numpy as jnp
from jax import lax

LAT = 64
STEPS = 2
K = 1296
LONW = 1024


def with_ends(array, key, smallest, largest):
    place = [jax.random.randint(jax.random.fold_in(key, axis), (), 0, length) for axis, length in enumerate(array.shape)]
    longest = array.shape.index(max(array.shape))
    neighbour = place[:longest] + [(place[longest] + 1) % array.shape[longest]] + place[longest + 1:]
    return array.at[tuple(place)].set(smallest).at[tuple(neighbour)].set(largest)


def steps_of(stream_key, dims, pieces, low, largest):
    def one(position, parts):
        steps = jax.random.uniform(jax.random.fold_in(jax.random.fold_in(stream_key, 6), position), (parts,), jnp.float32, low / len(pieces), largest / len(pieces))
        return jnp.repeat(jnp.exp(steps), dims[position] // parts).reshape((-1,) + (1,) * (len(dims) - position - 1))

    loudness = one(*pieces[0])
    for cut in pieces[1:]:
        loudness = loudness * one(*cut)
    return loudness


def bell_draw(own_key, extent, scale, most, cuts=(), dtype=jnp.bfloat16):
    loudness = steps_of(own_key, extent, cuts, -0.22, 0.18) if cuts else 1.0
    array = jax.random.normal(own_key, extent, jnp.float32) * scale * loudness
    return jnp.minimum(jnp.maximum(array, -most), most).astype(dtype)


def setup_inputs(seed: int = 0) -> dict:
    splits = jax.random.split(jax.random.key(seed), 9)
    lam_final = bell_draw(splits[0], (K, LAT, LONW), 1.0, 6.0, ((0, 4), (2, 8)), jnp.float32)
    stored_source = jnp.clip(0.19921875 + 0.99609375 * jax.random.uniform(splits[1], (STEPS, K, LAT, LONW), jnp.float32) ** steps_of(splits[1], (STEPS, K, LAT, LONW), ((1, 4), (3, 8)), -0.2, 0.2), 0.19921875, 1.1953125).astype(jnp.bfloat16)
    mixing = bell_draw(splits[2], (K, K), K ** -0.5, 0.15625)
    drift_x = jnp.clip(jax.random.uniform(splits[3], (K,), jnp.float32, -0.45, 0.45), -0.45, 0.45)
    drift_y = jnp.clip(jax.random.uniform(splits[4], (K,), jnp.float32, -0.45, 0.45), -0.45, 0.45)
    ocean_mask = with_ends((jax.random.randint(splits[5], (LAT, LONW), 0, 4) < 3).astype(jnp.int32), jax.random.fold_in(splits[5], 1), 0, 1)
    misfit = bell_draw(splits[6], (STEPS, LAT, LONW), 1.0, 6.0, ((2, 8),), jnp.float32)
    obs_mask = with_ends((jax.random.randint(splits[7], (STEPS, LAT, LONW), 0, 3) < 1).astype(jnp.int32), jax.random.fold_in(splits[7], 1), 0, 1)
    return {"lam_final": lam_final, "stored_source": stored_source, "mixing": mixing, "drift_x": drift_x, "drift_y": drift_y, "ocean_mask": ocean_mask, "misfit": misfit, "obs_mask": obs_mask}


def couple_terms(adjoint, mixing):
    rounded = adjoint.astype(jnp.bfloat16)
    flat = rounded.reshape(rounded.shape[0], -1).astype(jnp.float32)
    coupled = lax.dot_general(mixing.astype(jnp.float32), flat, (((0,), (0,)), ((), ())), precision=lax.Precision.HIGHEST, preferred_element_type=jnp.float32)
    coupled = lax.optimization_barrier(coupled.astype(jnp.bfloat16))
    return coupled.astype(jnp.float32).reshape(adjoint.shape)


def advect_back(adjoint, drift_x, drift_y):
    speed_x = drift_x[:, None, None]
    speed_y = drift_y[:, None, None]
    eastern = jnp.roll(adjoint, -1, axis=2)
    western = jnp.roll(adjoint, 1, axis=2)
    zero_row = jnp.zeros_like(adjoint[:, :1])
    northern = jnp.concatenate([adjoint[:, 1:], zero_row], axis=1)
    southern = jnp.concatenate([zero_row, adjoint[:, :-1]], axis=1)
    stay = 1.0 - jnp.abs(speed_x) - jnp.abs(speed_y)
    result = stay * adjoint + jnp.maximum(speed_x, 0.0) * eastern + jnp.maximum(-speed_x, 0.0) * western
    return result + jnp.maximum(speed_y, 0.0) * northern + jnp.maximum(-speed_y, 0.0) * southern


def reference(lam_final, stored_source, mixing, drift_x, drift_y, ocean_mask, misfit, obs_mask):
    ocean_field = ocean_mask.astype(jnp.float32)[None]
    adjoint = lam_final
    for step_index in reversed(range(STEPS)):
        forcing = misfit[step_index] * obs_mask[step_index].astype(jnp.float32)
        adjoint = (adjoint + forcing[None]) * ocean_field
        adjoint = adjoint + stored_source[step_index].astype(jnp.float32) * couple_terms(adjoint, mixing)
        adjoint = advect_back(adjoint, drift_x, drift_y)
    return adjoint
```

```python
import functools

import jax
import jax.numpy as jnp
from jax import lax
from jax.experimental import pallas as pl
from jax.experimental.pallas import tpu as pltpu
from jax.sharding import PartitionSpec as P

CHUNKS = 4
MESH = pl.DeviceIdType.MESH
F32, BF16 = jnp.float32, jnp.bfloat16


def round_up(value, unit):
    return -(-value // unit) * unit


class Plan:
    def __init__(self, steps, parts, ring, own, lat, width, base):
        self.steps, self.parts, self.ring = steps, parts, ring
        self.own, self.lat, self.width = own, lat, width
        self.rows = lat // parts
        self.base, self.over = base, self.rows - base
        self.lanes, self.spare = base * width, (self.rows - base) * width
        self.main = own // 16 * 16
        self.left = own - self.main
        self.pad = round_up(own, 16)
        edges = [self.main // 16 * q // CHUNKS * 16 for q in range(CHUNKS + 1)]
        self.bounds = list(zip(edges[:-1], edges[1:]))
        self.folded = round_up(base * self.left, 16)
        self.gathered = parts * self.main + parts * self.left

    def span(self, q):
        low, high = self.bounds[q]
        last = q == CHUNKS - 1
        held = high - low + (self.left if last else 0)
        return low, high - low, held, round_up(held, 16)

    @property
    def tallest(self):
        return max(self.span(q)[3] for q in range(CHUNKS))


def kernel(
    plan, lam, source, weight, drift_x, drift_y, ocean_mask, misfit, obs_mask, out,
    state, sin, rin, sout, rout, sin_l, rin_l, sout_l, rout_l,
    weight_buf, stage, source_buf, factor, coef, ocean, forcing, ids, fill, unfill, extra_in, extra_out, fold, mixed,
    halo_send, halo_recv,
    send_sem, recv_sem, left_send_sem, left_recv_sem, halo_send_sem, halo_recv_sem,
    stage_sem, source_sem, weight_sem, self_sem,
):
    me = lax.axis_index("spec")
    lon = lax.axis_index("lon")
    parts, ring, rows, lat, width = plan.parts, plan.ring, plan.rows, plan.lat, plan.width
    own, main, left, pad, lanes, base, over, spare = (
        plan.own, plan.main, plan.left, plan.pad, plan.lanes, plan.base, plan.over, plan.spare
    )
    steps, tallest = plan.steps, plan.tallest
    east, west = lax.rem(lon + 1, ring), lax.rem(lon + ring - 1, ring)
    peers = list(range(1, parts))
    order = [(step, q) for step in reversed(range(steps)) for q in range(CHUNKS)]
    lane = lax.broadcasted_iota(jnp.int32, (16, width), 1)

    def peer(offset):
        return lax.rem(me + offset, parts)

    def aligned(value):
        return pl.multiple_of(value, 16)

    def lam_copy(q):
        low, _, held, _ = plan.span(q)
        return pltpu.make_async_copy(
            lam.at[pl.ds(low * lat, held * lat)],
            stage.at[pl.ds((q % 2) * tallest * lat, held * lat)],
            stage_sem.at[q % 2],
        )

    def out_copy(q):
        low, _, held, _ = plan.span(q)
        return pltpu.make_async_copy(
            stage.at[pl.ds((q % 2) * tallest * lat, held * lat)],
            out.at[pl.ds(low * lat, held * lat)],
            stage_sem.at[q % 2],
        )

    def source_copy(position):
        step, q = order[position]
        low, _, held, _ = plan.span(q)
        return pltpu.make_async_copy(
            source.at[step, pl.ds(low, held)],
            source_buf.at[position % 2, pl.ds(0, held)],
            source_sem.at[position % 2],
        )

    weight_copy = pltpu.make_async_copy(weight, weight_buf, weight_sem)

    def inward(slot, q, offset):
        low, count, _, _ = plan.span(q)
        target = peer(offset)
        return pltpu.make_async_remote_copy(
            src_ref=sin.at[pl.ds(aligned(target * pad + low), count)],
            dst_ref=rin.at[slot, pl.ds(aligned(me * main + low), count)],
            send_sem=send_sem.at[0, q, offset],
            recv_sem=recv_sem.at[0, q, me],
            device_id={"spec": target},
            device_id_type=MESH,
        )

    def inward_arrival(slot, q, offset):
        low, count, _, _ = plan.span(q)
        origin = peer(offset)
        return pltpu.make_async_remote_copy(
            src_ref=sin.at[pl.ds(aligned(origin * pad + low), count)],
            dst_ref=rin.at[slot, pl.ds(aligned(origin * main + low), count)],
            send_sem=send_sem.at[0, q, offset],
            recv_sem=recv_sem.at[0, q, origin],
            device_id={"spec": origin},
            device_id_type=MESH,
        )

    def inward_self(slot, q):
        low, count, _, _ = plan.span(q)
        return pltpu.make_async_copy(
            sin.at[pl.ds(aligned(me * pad + low), count)],
            rin.at[slot, pl.ds(aligned(me * main + low), count)],
            self_sem.at[0, q],
        )

    def outward(q, offset):
        low, count, _, _ = plan.span(q)
        target = peer(offset)
        return pltpu.make_async_remote_copy(
            src_ref=sout.at[pl.ds(aligned(target * pad + low), count)],
            dst_ref=rout.at[pl.ds(aligned(me * pad + low), count)],
            send_sem=send_sem.at[1, q, offset],
            recv_sem=recv_sem.at[1, q, me],
            device_id={"spec": target},
            device_id_type=MESH,
        )

    def outward_arrival(q, offset):
        low, count, _, _ = plan.span(q)
        origin = peer(offset)
        return pltpu.make_async_remote_copy(
            src_ref=sout.at[pl.ds(aligned(origin * pad + low), count)],
            dst_ref=rout.at[pl.ds(aligned(origin * pad + low), count)],
            send_sem=send_sem.at[1, q, offset],
            recv_sem=recv_sem.at[1, q, origin],
            device_id={"spec": origin},
            device_id_type=MESH,
        )

    def outward_self(q):
        low, count, _, _ = plan.span(q)
        return pltpu.make_async_copy(
            sout.at[pl.ds(aligned(me * pad + low), count)],
            rout.at[pl.ds(aligned(me * pad + low), count)],
            self_sem.at[1, q],
        )

    def leftover(phase, offset, arriving):
        sender, receiver = (sin_l, rin_l) if phase == 0 else (sout_l, rout_l)
        other = peer(offset)
        place = other if arriving else me
        return pltpu.make_async_remote_copy(
            src_ref=sender.at[other],
            dst_ref=receiver.at[place],
            send_sem=left_send_sem.at[phase, offset],
            recv_sem=left_recv_sem.at[phase, place],
            device_id={"spec": other},
            device_id_type=MESH,
        )

    def halo(position, side):
        return pltpu.make_async_remote_copy(
            src_ref=halo_send.at[position, side],
            dst_ref=halo_recv.at[position, side],
            send_sem=halo_send_sem.at[position, side],
            recv_sem=halo_recv_sem.at[position, side],
            device_id={"lon": west if side == 0 else east},
            device_id_type=MESH,
        )

    for q in range(min(2, CHUNKS)):
        lam_copy(q).start()
    weight_copy.start()
    source_copy(0).start()
    source_copy(1).start()

    barrier = pltpu.get_barrier_semaphore()
    for offset in peers:
        pl.semaphore_signal(barrier, inc=1, device_id={"spec": peer(offset)}, device_id_type=MESH)
    for side in (west, east):
        pl.semaphore_signal(barrier, inc=1, device_id={"lon": side}, device_id_type=MESH)
    pl.semaphore_wait(barrier, len(peers) + 2)

    def set_forcing(step):
        forcing[...] = misfit[step] * obs_mask[step].astype(F32)

    wet = ocean_mask[...].astype(F32)
    ocean[...] = wet
    set_forcing(steps - 1)
    state[lat] = jnp.zeros((pad, width), F32)

    def column(row):
        return jnp.transpose(jnp.broadcast_to(ids[pl.ds(row, 1)], (width, width)))

    def match(tall, row):
        return jnp.where(tall == ids[pl.ds(row, 1)], 1.0, 0.0).astype(BF16)

    if over:
        row_of = lax.broadcasted_iota(jnp.int32, (lat, width), 0)

        def block_of(index):
            return sum((index >= b * rows).astype(jnp.int32) for b in range(1, parts))

        riding = row_of - block_of(row_of) * rows >= base
        chosen = jnp.where(riding, wet, 1.0 - wet)
        here = lax.broadcasted_iota(jnp.int32, (lat, lat), 0)
        there = lax.broadcasted_iota(jnp.int32, (lat, lat), 1)
        block_here, block_there = block_of(here), block_of(there)
        kind_here = (here - block_here * rows >= base).astype(jnp.int32)
        kind_there = (there - block_there * rows >= base).astype(jnp.int32)
        before = (block_here == block_there) & (kind_here == kind_there) & (there < here)
        first = lax.broadcasted_iota(jnp.int32, (width, width), 0)
        second = lax.broadcasted_iota(jnp.int32, (width, width), 1)
        packed = chosen.astype(BF16)
        within = jnp.dot(packed, (first < second).astype(F32).astype(BF16), preferred_element_type=F32)
        totals = jnp.dot(packed, jnp.ones((width, width), BF16), preferred_element_type=F32)
        offset_rows = jnp.dot(
            before.astype(F32).astype(BF16), totals.astype(BF16), preferred_element_type=F32
        )
        ids[...] = jnp.where(chosen > 0.0, within + offset_rows, jnp.where(riding, -1.0, -2.0))

        def fill_block(b, carry):
            for o in range(over):
                tall = column(b * rows + base + o)

                def one(r, inner):
                    fill[
                        pl.ds(pl.multiple_of(b * spare + o * width, width), width),
                        pl.ds(pl.multiple_of(r * width, width), width),
                    ] = match(tall, b * rows + r)
                    return inner

                lax.fori_loop(0, base, one, 0)
            return carry

        lax.fori_loop(0, parts, fill_block, 0)

    def emit(x, i, b, r, c, local):
        state[i, pl.ds(c, 16)] = x
        rounded = x.astype(BF16)
        if r < base:
            sin[pl.ds(aligned(b * pad + c), 16), r * width : (r + 1) * width] = rounded
        else:
            extra_in[b, pl.ds(local, 16), (r - base) * width : (r - base + 1) * width] = rounded

    def tiles(body):
        wide = lanes // (2 * width)

        def one(n, carry):
            body(pl.ds(pl.multiple_of(n * 2 * width, 2 * width), 2 * width))
            return carry

        lax.fori_loop(0, wide, one, 0)
        if wide * 2 * width < lanes:
            body(pl.ds(wide * 2 * width, width))

    def fold_rows(sender):
        def one(b, carry):
            value = sender[pl.ds(aligned(b * pad + main), 16), :].astype(F32)
            for t in range(base):
                fold[t * left : (t + 1) * left] = value[:left, t * width : (t + 1) * width]
            sin_l[b] = fold[...].astype(BF16)
            return carry

        lax.fori_loop(0, parts, one, 0)

    def send_inward(slot, q, first):
        low, count, held, tall = plan.span(q)
        last = q == CHUNKS - 1
        if over:

            def block(b, carry):
                place = pl.ds(aligned(b * pad + low), tall)

                def one(cols):
                    moved = jnp.dot(
                        extra_in[b, :tall],
                        fill[pl.ds(pl.multiple_of(b * spare, width), spare), cols],
                        preferred_element_type=F32,
                    )
                    sin[place, cols] = (sin[place, cols].astype(F32) + moved).astype(BF16)

                tiles(one)
                return carry

            lax.fori_loop(0, parts, block, 0)
        inward_self(slot, q).start()
        for offset in peers:
            inward(slot, q, offset).start()
        if last and left:
            if not first:
                for offset in peers:
                    leftover(0, offset, False).wait_send()
            fold_rows(sin)
            for offset in peers:
                leftover(0, offset, False).start()
            rin_l[me] = sin_l[me]

    for q in range(CHUNKS):
        low, count, held, tall = plan.span(q)
        lam_copy(q).wait()
        start = (q % 2) * tallest * lat

        def prepare(g, carry):
            def block(b, inner):
                for r in range(rows):
                    i = b * rows + r
                    a = stage[pl.ds(start + g * 16 * lat + i, 16, stride=lat)]
                    x = (a + forcing[pl.ds(i, 1)]) * ocean[pl.ds(i, 1)]
                    emit(x, i, b, r, aligned(low + g * 16), aligned(g * 16))
                return inner

            return lax.fori_loop(0, parts, block, carry)

        lax.fori_loop(0, tall // 16, prepare, 0)
        if q + 2 < CHUNKS:
            lam_copy(q + 2).start()
        send_inward((steps - 1) % 2, q, True)

    def coefficients(c, carry):
        speed_x = drift_x[me * own + c]
        speed_y = drift_y[me * own + c]
        values = (
            1.0 - jnp.abs(speed_x) - jnp.abs(speed_y),
            jnp.maximum(speed_x, 0.0), jnp.maximum(-speed_x, 0.0),
            jnp.maximum(speed_y, 0.0), jnp.maximum(-speed_y, 0.0),
        )
        for k, value in enumerate(values):
            coef[k, pl.ds(c, 1)] = jnp.full((1, width), value, F32)
        return carry

    lax.fori_loop(0, own, coefficients, 0)

    if over:

        def unfill_block(b, carry):
            def one(r, inner):
                tall = column(b * rows + r)
                for o in range(over):
                    unfill[
                        pl.ds(pl.multiple_of((b * base + r) * width, width), width), o * width : (o + 1) * width
                    ] = match(tall, b * rows + base + o)
                return inner

            return lax.fori_loop(0, base, one, carry)

        lax.fori_loop(0, parts, unfill_block, 0)
    weight_copy.wait()

    for step in reversed(range(steps)):
        final = step == 0
        first = step == steps - 1
        slot = step % 2

        for q in range(CHUNKS):
            inward_self(slot, q).wait()
            for offset in peers:
                inward_arrival(slot, q, offset).wait_recv()
        if left:
            for offset in peers:
                leftover(0, offset, True).wait_recv()
            for o in range(parts):
                value = rin_l[o].astype(F32)
                for t in range(base):
                    mixed[o * left : (o + 1) * left, t * width : (t + 1) * width] = value[t * left : (t + 1) * left]
            rin[slot, parts * main :] = mixed[...].astype(BF16)

        start = 0
        for q in range(CHUNKS):
            low, count, held, tall = plan.span(q)
            last = q == CHUNKS - 1
            if not first:
                for offset in peers:
                    outward(q, offset).wait_send()

            def couple(cols):
                result = jnp.dot(
                    weight_buf[start : start + parts * count], rin[slot, :, cols], preferred_element_type=F32
                )
                for h in range(parts):
                    sout[h * pad + low : h * pad + low + count, cols] = result[h * count : (h + 1) * count].astype(BF16)

            tiles(couple)
            outward_self(q).start()
            for offset in peers:
                outward(q, offset).start()
            start += parts * count
            if last and left:
                if not first:
                    for offset in peers:
                        leftover(1, offset, False).wait_send()

                def couple_left(cols):
                    mixed[:, cols] = jnp.dot(weight_buf[start:], rin[slot, :, cols], preferred_element_type=F32)

                tiles(couple_left)
                for h in range(parts):
                    for t in range(base):
                        fold[t * left : (t + 1) * left] = mixed[
                            h * left : (h + 1) * left, t * width : (t + 1) * width
                        ]
                    sout_l[h] = fold[...].astype(BF16)
                for offset in peers:
                    leftover(1, offset, False).start()
                rout_l[me] = sout_l[me]

        if not final:
            set_forcing(step - 1)
        for q in range(CHUNKS):
            low, count, held, tall = plan.span(q)
            last = q == CHUNKS - 1
            position = (steps - 1 - step) * CHUNKS + q
            source_slot = position % 2
            source_copy(position).wait()
            outward_self(q).wait()
            for offset in peers:
                outward_arrival(q, offset).wait_recv()
            if last and left:
                for offset in peers:
                    leftover(1, offset, True).wait_recv()

                def spread(b, carry):
                    value = rout_l[b].astype(F32)
                    for t in range(base):
                        mixed[:left, t * width : (t + 1) * width] = value[t * left : (t + 1) * left]
                    rout[pl.ds(aligned(b * pad + main), 16)] = mixed[...].astype(BF16)
                    return carry

                lax.fori_loop(0, parts, spread, 0)
            if over:

                def restore(b, carry):
                    extra_out[b, :tall] = jnp.dot(
                        rout[pl.ds(aligned(b * pad + low), tall)],
                        unfill[pl.ds(pl.multiple_of(b * lanes, width), lanes)],
                        preferred_element_type=F32,
                    )
                    return carry

                lax.fori_loop(0, parts, restore, 0)

            def update(g, carry):
                c = aligned(low + g * 16)
                local = aligned(g * 16)
                for k in range(16):
                    factor[k * lat : (k + 1) * lat] = source_buf[source_slot, local + k].astype(F32)

                def block(b, edges):
                    to_west, to_east = edges
                    for r in range(rows):
                        i = b * rows + r
                        if r < base:
                            coupled = rout[
                                pl.ds(aligned(b * pad + c), 16), r * width : (r + 1) * width
                            ].astype(F32)
                            if over:
                                coupled = coupled * ocean[pl.ds(i, 1)]
                        else:
                            coupled = extra_out[b, pl.ds(local, 16), (r - base) * width : (r - base + 1) * width]
                        adjoint = state[i, pl.ds(c, 16)] + factor[pl.ds(i, 16, stride=lat)] * coupled
                        state[i, pl.ds(c, 16)] = adjoint
                        to_west = jnp.where(lane == 0, adjoint, pltpu.roll(to_west, 1, 1))
                        to_east = jnp.where(lane == width - 1, adjoint, pltpu.roll(to_east, width - 1, 1))
                    return to_west, to_east

                zero = jnp.zeros((16, width), F32)
                to_west, to_east = lax.fori_loop(0, parts, block, (zero, zero))
                halo_send[position, 0, pl.ds(local, 16)] = to_west
                halo_send[position, 1, pl.ds(local, 16)] = to_east
                return carry

            lax.fori_loop(0, tall // 16, update, 0)
            halo(position, 0).start()
            halo(position, 1).start()
            if position + 2 < len(order):
                source_copy(position + 2).start()
            if final:
                if q >= 2:
                    out_copy(q - 2).wait()
            else:
                for offset in peers:
                    inward(slot, q, offset).wait_send()
            halo(position, 0).wait()
            halo(position, 1).wait()
            begin = (q % 2) * tallest * lat

            def advect(g, carry):
                c = aligned(low + g * 16)
                local = aligned(g * 16)
                stay, px, nx, py, ny = (coef[k, pl.ds(c, 16)] for k in range(5))

                def block(b, state_of):
                    southern, adjoint, from_east, from_west = state_of
                    for r in range(rows):
                        i = b * rows + r
                        northern = state[i + 1, pl.ds(c, 16)]
                        eastern = jnp.where(lane == width - 1, from_east, pltpu.roll(adjoint, width - 1, 1))
                        western = jnp.where(lane == 0, from_west, pltpu.roll(adjoint, 1, 1))
                        result = stay * adjoint + px * eastern + nx * western
                        result = result + py * northern + ny * southern
                        if final:
                            stage[pl.ds(begin + local * lat + i, 16, stride=lat)] = result
                        else:
                            emit((result + forcing[pl.ds(i, 1)]) * ocean[pl.ds(i, 1)], i, b, r, c, local)
                        southern, adjoint = adjoint, northern
                        from_east, from_west = pltpu.roll(from_east, 1, 1), pltpu.roll(from_west, width - 1, 1)
                    return southern, adjoint, from_east, from_west

                lax.fori_loop(
                    0, parts, block,
                    (
                        jnp.zeros((16, width), F32),
                        state[0, pl.ds(c, 16)],
                        pltpu.roll(halo_recv[position, 0, pl.ds(local, 16)], (width - lat) % width, 1),
                        pltpu.roll(halo_recv[position, 1, pl.ds(local, 16)], lat % width, 1),
                    ),
                )
                return carry

            lax.fori_loop(0, tall // 16, advect, 0)
            if final:
                out_copy(q).start()
            else:
                send_inward((step - 1) % 2, q, False)

    for q in range(CHUNKS):
        for offset in peers:
            inward(0, q, offset).wait_send()
            outward(q, offset).wait_send()
    if left:
        for offset in peers:
            leftover(0, offset, False).wait_send()
            leftover(1, offset, False).wait_send()
    for q in range(max(CHUNKS - 2, 0), CHUNKS):
        out_copy(q).wait()


def call(plan, identity, lam, source, weight, drift_x, drift_y, ocean_mask, misfit, obs_mask):
    vmem = pl.BlockSpec(memory_space=pltpu.VMEM)
    smem = pl.BlockSpec(memory_space=pltpu.SMEM)
    hbm = pl.BlockSpec(memory_space=pl.ANY)
    dma = pltpu.SemaphoreType.DMA
    parts, pad, lanes, lat, width = plan.parts, plan.pad, plan.lanes, plan.lat, plan.width
    tallest = plan.tallest
    positions = plan.steps * CHUNKS
    spare = max(plan.spare, width)
    filling = (parts * spare, lanes) if plan.over else (16, width)
    unfilling = (parts * lanes, spare) if plan.over else (16, width)
    folded = max(plan.folded, 16)
    left = (parts, folded, width)
    return pl.pallas_call(
        functools.partial(kernel, plan),
        out_shape=jax.ShapeDtypeStruct((plan.own * lat, width), F32),
        in_specs=[hbm, hbm, hbm, smem, smem, vmem, vmem, vmem],
        out_specs=hbm,
        scratch_shapes=[
            pltpu.VMEM((lat + 1, pad, width), F32),
            pltpu.VMEM((parts * pad, lanes), BF16),
            pltpu.VMEM((2, plan.gathered, lanes), BF16),
            pltpu.VMEM((parts * pad, lanes), BF16),
            pltpu.VMEM((parts * pad, lanes), BF16),
            pltpu.VMEM(left, BF16), pltpu.VMEM(left, BF16), pltpu.VMEM(left, BF16), pltpu.VMEM(left, BF16),
            pltpu.VMEM(weight.shape, BF16),
            pltpu.VMEM((2 * tallest * lat, width), F32),
            pltpu.VMEM((2, tallest, lat, width), BF16),
            pltpu.VMEM((16 * lat, width), F32),
            pltpu.VMEM((5, pad, width), F32),
            pltpu.VMEM((lat, width), F32),
            pltpu.VMEM((lat, width), F32),
            pltpu.VMEM((lat, width), F32),
            pltpu.VMEM(filling, BF16),
            pltpu.VMEM(unfilling, BF16),
            pltpu.VMEM((parts, tallest, spare), BF16),
            pltpu.VMEM((parts, tallest, spare), F32),
            pltpu.VMEM((folded, width), F32),
            pltpu.VMEM((16, lanes), F32),
            pltpu.VMEM((positions, 2, tallest, width), F32),
            pltpu.VMEM((positions, 2, tallest, width), F32),
            dma((2, CHUNKS, parts)),
            dma((2, CHUNKS, parts)),
            dma((2, parts)),
            dma((2, parts)),
            dma((positions, 2)),
            dma((positions, 2)),
            dma((2,)),
            dma((2,)),
            dma,
            dma((2, CHUNKS)),
        ],
        compiler_params=pltpu.CompilerParams(
            collective_id=identity, has_side_effects=True, vmem_limit_bytes=62 * 1024 * 1024
        ),
    )(lam, source, weight, drift_x, drift_y, ocean_mask, misfit, obs_mask)


def census_kernel(ring, parts, ocean_mask, most, mine, others, send_sem, recv_sem):
    lon = lax.axis_index("lon")
    rows = ocean_mask.shape[0] // parts
    barrier = pltpu.get_barrier_semaphore()
    for k in range(1, ring):
        pl.semaphore_signal(barrier, inc=1, device_id={"lon": lax.rem(lon + k, ring)}, device_id_type=MESH)
    worst = jnp.zeros((8, 128), F32)
    for b in range(parts):
        count = jnp.sum(ocean_mask[b * rows : (b + 1) * rows].astype(F32))
        worst = jnp.maximum(worst, jnp.full((8, 128), count, F32))
    mine[...] = worst
    pl.semaphore_wait(barrier, ring - 1)

    def copy(k, arriving):
        other = lax.rem(lon + k, ring)
        place = other if arriving else lon
        return pltpu.make_async_remote_copy(
            src_ref=mine,
            dst_ref=others.at[place],
            send_sem=send_sem.at[k],
            recv_sem=recv_sem.at[place],
            device_id={"lon": other},
            device_id_type=MESH,
        )

    for k in range(1, ring):
        copy(k, False).start()
    for k in range(1, ring):
        copy(k, True).wait_recv()
        worst = jnp.maximum(worst, others[lax.rem(lon + k, ring)])
    for k in range(1, ring):
        copy(k, False).wait_send()
    most[...] = worst


def census(ring, parts, ocean_mask):
    vmem = pl.BlockSpec(memory_space=pltpu.VMEM)
    return pl.pallas_call(
        functools.partial(census_kernel, ring, parts),
        out_shape=jax.ShapeDtypeStruct((8, 128), F32),
        in_specs=[vmem],
        out_specs=vmem,
        scratch_shapes=[
            pltpu.VMEM((8, 128), F32),
            pltpu.VMEM((ring, 8, 128), F32),
            pltpu.SemaphoreType.DMA((ring,)),
            pltpu.SemaphoreType.DMA((ring,)),
        ],
        compiler_params=pltpu.CompilerParams(collective_id=0, has_side_effects=True),
    )(ocean_mask)


def arrange(plan, mixing):
    own, main, parts = plan.own, plan.main, plan.parts
    gathered = jnp.concatenate(
        [mixing[o * own : o * own + main] for o in range(parts)]
        + [mixing[o * own + main : (o + 1) * own] for o in range(parts)],
        axis=0,
    )
    columns = [
        gathered[:, h * own + low : h * own + high] for low, high in plan.bounds for h in range(parts)
    ] + [gathered[:, h * own + main : (h + 1) * own] for h in range(parts)]
    return jnp.concatenate(columns, axis=1).T


def per_device(
    parts, ring, lam_final, stored_source, mixing, drift_x, drift_y, ocean_mask, misfit, obs_mask
):
    steps = stored_source.shape[0]
    own, lat, width = lam_final.shape
    rows = lat // parts
    packed = Plan(steps, parts, ring, own, lat, width, -(-rows * 13 // 16))
    whole = Plan(steps, parts, ring, own, lat, width, rows)
    weight = arrange(whole, mixing)
    most = census(ring, parts, ocean_mask)
    operands = (
        lam_final.reshape(own * lat, width), stored_source, weight, drift_x, drift_y, ocean_mask, misfit, obs_mask
    )
    result = lax.cond(
        most[0, 0] <= packed.lanes,
        functools.partial(call, packed, 1),
        functools.partial(call, whole, 2),
        *operands,
    )
    return result.reshape(own, lat, width)


def solution(mesh):
    in_specs = (
        P("spec", None, "lon"),
        P(None, "spec", None, "lon"),
        P(),
        P(),
        P(),
        P(None, "lon"),
        P(None, None, "lon"),
        P(None, None, "lon"),
    )
    out_specs = P("spec", None, "lon")
    return jax.shard_map(
        functools.partial(per_device, mesh.shape["spec"], mesh.shape["lon"]),
        mesh=mesh, in_specs=in_specs, out_specs=out_specs, check_vma=False,
    )
```

```python
import functools

import jax
import jax.numpy as jnp
from jax import lax
from jax.experimental import pallas as pl
from jax.experimental.pallas import tpu as pltpu
from jax.sharding import PartitionSpec as P

CHUNKS = 5
MESH = pl.DeviceIdType.MESH
F32, BF16 = jnp.float32, jnp.bfloat16


def round_up(value, unit):
    return -(-value // unit) * unit


class Plan:
    def __init__(self, steps, parts, ring, own, lat, width, base):
        self.steps, self.parts, self.ring = steps, parts, ring
        self.own, self.lat, self.width = own, lat, width
        self.rows = lat // parts
        self.base, self.over = base, self.rows - base
        self.lanes, self.spare = base * width, (self.rows - base) * width
        self.main = own // 16 * 16
        self.left = own - self.main
        self.pad = round_up(own, 16)
        groups = self.pad // 16
        edges = [(groups * q + CHUNKS // 2) // CHUNKS * 16 for q in range(CHUNKS)] + [self.main]
        self.bounds = list(zip(edges[:-1], edges[1:]))
        self.folded = round_up(base * self.left, 16)

    def span(self, q):
        low, high = self.bounds[q]
        last = q == CHUNKS - 1
        held = high - low + (self.left if last else 0)
        return low, high - low, held, round_up(held, 16)

    @property
    def tallest(self):
        return max(self.span(q)[3] for q in range(CHUNKS))


def kernel(
    plan, lam, source, mixing, drift_x, drift_y, ocean_mask, misfit, obs_mask, out,
    state, sin, rin, sout, rout, sin_l, rin_l, sout_l, rout_l,
    weight_buf, mixing_buf, stage, source_buf, factor, coef, ocean, forcing, ids, fill, unfill, extra_in, extra_out, fold, mixed, lift,
    halo_send, halo_recv,
    send_sem, recv_sem, left_send_sem, left_recv_sem, halo_send_sem, halo_recv_sem,
    stage_sem, source_sem, weight_sem, self_sem,
):
    me = lax.axis_index("spec")
    lon = lax.axis_index("lon")
    parts, ring, rows, lat, width = plan.parts, plan.ring, plan.rows, plan.lat, plan.width
    own, main, left, pad, lanes, base, over, spare = (
        plan.own, plan.main, plan.left, plan.pad, plan.lanes, plan.base, plan.over, plan.spare
    )
    steps, tallest = plan.steps, plan.tallest
    east, west = lax.rem(lon + 1, ring), lax.rem(lon + ring - 1, ring)
    peers = list(range(1, parts))
    order = [(step, q) for step in reversed(range(steps)) for q in range(CHUNKS)]
    lane = lax.broadcasted_iota(jnp.int32, (16, width), 1)

    def peer(offset):
        return lax.rem(me + offset, parts)

    def aligned(value):
        return pl.multiple_of(value, 16)

    def lam_copy(q):
        low, _, held, _ = plan.span(q)
        return pltpu.make_async_copy(
            lam.at[pl.ds(low * lat, held * lat)],
            stage.at[pl.ds((q % 2) * tallest * lat, held * lat)],
            stage_sem.at[q % 2],
        )

    def out_copy(q):
        low, _, held, _ = plan.span(q)
        return pltpu.make_async_copy(
            stage.at[pl.ds((q % 2) * tallest * lat, held * lat)],
            out.at[pl.ds(low * lat, held * lat)],
            stage_sem.at[q % 2],
        )

    def source_copy(position):
        step, q = order[position]
        low, _, held, _ = plan.span(q)
        return pltpu.make_async_copy(
            source.at[step, pl.ds(low, held)],
            source_buf.at[position % 2, pl.ds(0, held)],
            source_sem.at[position % 2],
        )

    mixing_copy = pltpu.make_async_copy(mixing, mixing_buf.at[pl.ds(0, parts * own)], weight_sem)

    def inward(slot, q, offset):
        low, count, _, _ = plan.span(q)
        target = peer(offset)
        return pltpu.make_async_remote_copy(
            src_ref=sin.at[pl.ds(aligned(target * pad + low), count)],
            dst_ref=rin.at[slot, pl.ds(aligned(me * pad + low), count)],
            send_sem=send_sem.at[0, q, offset],
            recv_sem=recv_sem.at[0, q, me],
            device_id={"spec": target},
            device_id_type=MESH,
        )

    def inward_arrival(slot, q, offset):
        low, count, _, _ = plan.span(q)
        origin = peer(offset)
        return pltpu.make_async_remote_copy(
            src_ref=sin.at[pl.ds(aligned(origin * pad + low), count)],
            dst_ref=rin.at[slot, pl.ds(aligned(origin * pad + low), count)],
            send_sem=send_sem.at[0, q, offset],
            recv_sem=recv_sem.at[0, q, origin],
            device_id={"spec": origin},
            device_id_type=MESH,
        )

    def inward_self(slot, q):
        low, count, _, _ = plan.span(q)
        return pltpu.make_async_copy(
            sin.at[pl.ds(aligned(me * pad + low), count)],
            rin.at[slot, pl.ds(aligned(me * pad + low), count)],
            self_sem.at[0, q],
        )

    def outward(q, offset):
        low, count, _, _ = plan.span(q)
        target = peer(offset)
        return pltpu.make_async_remote_copy(
            src_ref=sout.at[pl.ds(aligned(target * pad + low), count)],
            dst_ref=rout.at[pl.ds(aligned(me * pad + low), count)],
            send_sem=send_sem.at[1, q, offset],
            recv_sem=recv_sem.at[1, q, me],
            device_id={"spec": target},
            device_id_type=MESH,
        )

    def outward_arrival(q, offset):
        low, count, _, _ = plan.span(q)
        origin = peer(offset)
        return pltpu.make_async_remote_copy(
            src_ref=sout.at[pl.ds(aligned(origin * pad + low), count)],
            dst_ref=rout.at[pl.ds(aligned(origin * pad + low), count)],
            send_sem=send_sem.at[1, q, offset],
            recv_sem=recv_sem.at[1, q, origin],
            device_id={"spec": origin},
            device_id_type=MESH,
        )

    def outward_self(q):
        low, count, _, _ = plan.span(q)
        return pltpu.make_async_copy(
            sout.at[pl.ds(aligned(me * pad + low), count)],
            rout.at[pl.ds(aligned(me * pad + low), count)],
            self_sem.at[1, q],
        )

    def leftover(phase, offset, arriving):
        sender, receiver = (sin_l, rin_l) if phase == 0 else (sout_l, rout_l)
        other = peer(offset)
        place = other if arriving else me
        return pltpu.make_async_remote_copy(
            src_ref=sender.at[other],
            dst_ref=receiver.at[place],
            send_sem=left_send_sem.at[phase, offset],
            recv_sem=left_recv_sem.at[phase, place],
            device_id={"spec": other},
            device_id_type=MESH,
        )

    def halo(position, side):
        return pltpu.make_async_remote_copy(
            src_ref=halo_send.at[position],
            dst_ref=halo_recv.at[position, side],
            send_sem=halo_send_sem.at[position, side],
            recv_sem=halo_recv_sem.at[position, side],
            device_id={"lon": west if side == 0 else east},
            device_id_type=MESH,
        )

    for q in range(min(2, CHUNKS)):
        lam_copy(q).start()
    mixing_copy.start()
    source_copy(0).start()
    source_copy(1).start()

    barrier = pltpu.get_barrier_semaphore()
    for offset in peers:
        pl.semaphore_signal(barrier, inc=1, device_id={"spec": peer(offset)}, device_id_type=MESH)
    for side in (west, east):
        pl.semaphore_signal(barrier, inc=1, device_id={"lon": side}, device_id_type=MESH)
    pl.semaphore_wait(barrier, len(peers) + 2)

    def set_forcing(step):
        forcing[...] = misfit[step] * obs_mask[step].astype(F32)

    wet = ocean_mask[...].astype(F32)
    ocean[...] = wet
    set_forcing(steps - 1)
    state[lat] = jnp.zeros((pad, width), F32)
    if left:
        lift[...] = jnp.zeros((16, lanes), F32)

    def column(row):
        return jnp.transpose(jnp.broadcast_to(ids[pl.ds(row, 1)], (width, width)))

    def match(tall, row):
        return jnp.where(tall == ids[pl.ds(row, 1)], 1.0, 0.0).astype(BF16)

    if over:
        row_of = lax.broadcasted_iota(jnp.int32, (lat, width), 0)

        def block_of(index):
            return sum((index >= b * rows).astype(jnp.int32) for b in range(1, parts))

        riding = row_of - block_of(row_of) * rows >= base
        chosen = jnp.where(riding, wet, 1.0 - wet)
        here = lax.broadcasted_iota(jnp.int32, (lat, lat), 0)
        there = lax.broadcasted_iota(jnp.int32, (lat, lat), 1)
        block_here, block_there = block_of(here), block_of(there)
        kind_here = (here - block_here * rows >= base).astype(jnp.int32)
        kind_there = (there - block_there * rows >= base).astype(jnp.int32)
        before = (block_here == block_there) & (kind_here == kind_there) & (there < here)
        first = lax.broadcasted_iota(jnp.int32, (width, width), 0)
        second = lax.broadcasted_iota(jnp.int32, (width, width), 1)
        packed = chosen.astype(BF16)
        within = jnp.dot(packed, (first < second).astype(F32).astype(BF16), preferred_element_type=F32)
        totals = jnp.dot(packed, jnp.ones((width, width), BF16), preferred_element_type=F32)
        offset_rows = jnp.dot(
            before.astype(F32).astype(BF16), totals.astype(BF16), preferred_element_type=F32
        )
        ids[...] = jnp.where(chosen > 0.0, within + offset_rows, jnp.where(riding, -1.0, -2.0))

        def fill_block(b, carry):
            for o in range(over):
                tall = column(b * rows + base + o)

                def one(r, inner):
                    fill[
                        pl.ds(pl.multiple_of(b * spare + o * width, width), width),
                        pl.ds(pl.multiple_of(r * width, width), width),
                    ] = match(tall, b * rows + r)
                    return inner

                lax.fori_loop(0, base, one, 0)
            return carry

        lax.fori_loop(0, parts, fill_block, 0)

    def emit(x, i, b, r, c, local):
        state[i, pl.ds(c, 16)] = x
        rounded = x.astype(BF16)
        if r < base:
            sin[pl.ds(aligned(b * pad + c), 16), r * width : (r + 1) * width] = rounded
        else:
            extra_in[b, pl.ds(local, 16), (r - base) * width : (r - base + 1) * width] = rounded

    def tiles(body):
        wide = lanes // (2 * width)

        def one(n, carry):
            body(pl.ds(pl.multiple_of(n * 2 * width, 2 * width), 2 * width))
            return carry

        lax.fori_loop(0, wide, one, 0)
        if wide * 2 * width < lanes:
            body(pl.ds(wide * 2 * width, width))

    def fold_rows(sender):
        def one(b, carry):
            value = sender[pl.ds(aligned(b * pad + main), 16), :].astype(F32)
            for t in range(base):
                fold[t * left : (t + 1) * left] = value[:left, t * width : (t + 1) * width]
            sin_l[b] = fold[...].astype(BF16)
            return carry

        lax.fori_loop(0, parts, one, 0)

    def send_inward(slot, q, first):
        low, count, held, tall = plan.span(q)
        last = q == CHUNKS - 1
        if over:

            def block(b, carry):
                place = pl.ds(aligned(b * pad + low), tall)

                def one(cols):
                    moved = jnp.dot(
                        extra_in[b, :tall],
                        fill[pl.ds(pl.multiple_of(b * spare, width), spare), cols],
                        preferred_element_type=F32,
                    )
                    sin[place, cols] = (sin[place, cols].astype(F32) + moved).astype(BF16)

                tiles(one)
                return carry

            lax.fori_loop(0, parts, block, 0)
        inward_self(slot, q).start()
        for offset in peers:
            inward(slot, q, offset).start()
        if last and left:
            if not first:
                for offset in peers:
                    leftover(0, offset, False).wait_send()
            fold_rows(sin)
            for offset in peers:
                leftover(0, offset, False).start()
            rin_l[me] = sin_l[me]

    for q in range(CHUNKS):
        low, count, held, tall = plan.span(q)
        lam_copy(q).wait()
        start = (q % 2) * tallest * lat

        def prepare(g, carry):
            def block(b, inner):
                for r in range(rows):
                    i = b * rows + r
                    a = stage[pl.ds(start + g * 16 * lat + i, 16, stride=lat)]
                    x = (a + forcing[pl.ds(i, 1)]) * ocean[pl.ds(i, 1)]
                    emit(x, i, b, r, aligned(low + g * 16), aligned(g * 16))
                return inner

            return lax.fori_loop(0, parts, block, carry)

        lax.fori_loop(0, tall // 16, prepare, 0)
        if q + 2 < CHUNKS:
            lam_copy(q + 2).start()
        send_inward((steps - 1) % 2, q, True)

    def coefficients(c, carry):
        speed_x = drift_x[me * own + c]
        speed_y = drift_y[me * own + c]
        values = (
            1.0 - jnp.abs(speed_x) - jnp.abs(speed_y),
            jnp.maximum(speed_x, 0.0), jnp.maximum(-speed_x, 0.0),
            jnp.maximum(speed_y, 0.0), jnp.maximum(-speed_y, 0.0),
        )
        for k, value in enumerate(values):
            coef[k, pl.ds(c, 1)] = jnp.full((1, width), value, F32)
        return carry

    lax.fori_loop(0, own, coefficients, 0)

    if over:

        def unfill_block(b, carry):
            def one(r, inner):
                tall = column(b * rows + r)
                for o in range(over):
                    unfill[
                        pl.ds(pl.multiple_of((b * base + r) * width, width), width), o * width : (o + 1) * width
                    ] = match(tall, b * rows + base + o)
                return inner

            return lax.fori_loop(0, base, one, carry)

        lax.fori_loop(0, parts, unfill_block, 0)

    mixing_copy.wait()

    def arrange_weights():
        wide = mixing_buf.shape[0]
        start = 0
        pieces = [plan.bounds[q] for q in range(CHUNKS)] + ([(main, pad)] if left else [])
        for low, high in pieces:
            count = high - low
            picked = lax.broadcasted_iota(jnp.int32, (count, parts * own), 0) + low
            picking = lax.broadcasted_iota(jnp.int32, (count, parts * own), 1)
            place = lax.broadcasted_iota(jnp.int32, (count, wide), 1)

            def one(h, carry):
                pick = (picking == h * own + picked) & (picked < own)
                rows_of_home = lax.dot_general(
                    pick.astype(F32).astype(BF16), mixing_buf[...], (((1,), (1,)), ((), ())),
                    preferred_element_type=F32,
                )
                value = jnp.zeros((count, wide), F32)
                for o in range(parts):
                    shifted = pltpu.roll(rows_of_home, o * (pad - own), 1) if o and pad > own else rows_of_home
                    value = jnp.where((place >= o * pad) & (place < o * pad + own), shifted, value)
                weight_buf[pl.ds(aligned(start + h * count), count)] = value.astype(BF16)[:, : parts * pad]
                return carry

            lax.fori_loop(0, parts, one, 0)
            start += parts * count

    arrange_weights()

    for step in reversed(range(steps)):
        final = step == 0
        first = step == steps - 1
        slot = step % 2

        for q in range(CHUNKS):
            inward_self(slot, q).wait()
            for offset in peers:
                inward_arrival(slot, q, offset).wait_recv()
        if left:
            for offset in peers:
                leftover(0, offset, True).wait_recv()

            def lift_rows(o, carry):
                value = rin_l[o].astype(F32)
                for t in range(base):
                    lift[:left, t * width : (t + 1) * width] = value[t * left : (t + 1) * left]
                rin[slot, pl.ds(aligned(o * pad + main), 16)] = lift[...].astype(BF16)
                return carry

            lax.fori_loop(0, parts, lift_rows, 0)

        start = 0
        for q in range(CHUNKS):
            low, count, held, tall = plan.span(q)
            last = q == CHUNKS - 1
            if not first:
                for offset in peers:
                    outward(q, offset).wait_send()

            def couple(cols):
                result = jnp.dot(
                    weight_buf[start : start + parts * count], rin[slot, :, cols], preferred_element_type=F32
                )
                for h in range(parts):
                    sout[h * pad + low : h * pad + low + count, cols] = result[h * count : (h + 1) * count].astype(BF16)

            tiles(couple)
            outward_self(q).start()
            for offset in peers:
                outward(q, offset).start()
            start += parts * count
            if last and left:
                if not first:
                    for offset in peers:
                        leftover(1, offset, False).wait_send()

                def couple_left(cols):
                    mixed[:, cols] = jnp.dot(
                        weight_buf[start : start + parts * 16], rin[slot, :, cols], preferred_element_type=F32
                    )

                tiles(couple_left)
                for h in range(parts):
                    for t in range(base):
                        fold[t * left : (t + 1) * left] = mixed[
                            h * 16 : h * 16 + left, t * width : (t + 1) * width
                        ]
                    sout_l[h] = fold[...].astype(BF16)
                for offset in peers:
                    leftover(1, offset, False).start()
                rout_l[me] = sout_l[me]

        if not final:
            set_forcing(step - 1)
        for q in range(CHUNKS):
            low, count, held, tall = plan.span(q)
            last = q == CHUNKS - 1
            position = (steps - 1 - step) * CHUNKS + q
            source_slot = position % 2
            source_copy(position).wait()
            outward_self(q).wait()
            for offset in peers:
                outward_arrival(q, offset).wait_recv()
            if last and left:
                for offset in peers:
                    leftover(1, offset, True).wait_recv()

                def spread(b, carry):
                    value = rout_l[b].astype(F32)
                    for t in range(base):
                        lift[:left, t * width : (t + 1) * width] = value[t * left : (t + 1) * left]
                    rout[pl.ds(aligned(b * pad + main), 16)] = lift[...].astype(BF16)
                    return carry

                lax.fori_loop(0, parts, spread, 0)
            if over:

                def restore(b, carry):
                    extra_out[b, :tall] = jnp.dot(
                        rout[pl.ds(aligned(b * pad + low), tall)],
                        unfill[pl.ds(pl.multiple_of(b * lanes, width), lanes)],
                        preferred_element_type=F32,
                    )
                    return carry

                lax.fori_loop(0, parts, restore, 0)

            def update(g, carry):
                c = aligned(low + g * 16)
                local = aligned(g * 16)
                for k in range(16):
                    factor[k * lat : (k + 1) * lat] = source_buf[source_slot, local + k].astype(F32)

                def block(b, edges):
                    ends = edges
                    for r in range(rows):
                        i = b * rows + r
                        if r < base:
                            coupled = rout[
                                pl.ds(aligned(b * pad + c), 16), r * width : (r + 1) * width
                            ].astype(F32)
                            if over:
                                coupled = coupled * ocean[pl.ds(i, 1)]
                        else:
                            coupled = extra_out[b, pl.ds(local, 16), (r - base) * width : (r - base + 1) * width]
                        adjoint = state[i, pl.ds(c, 16)] + factor[pl.ds(i, 16, stride=lat)] * coupled
                        state[i, pl.ds(c, 16)] = adjoint
                        place = lane - 2 * i
                        ends = jnp.where((place == 0) | (place == 1), pltpu.roll(adjoint, 2 * i + 1, 1), ends)
                    return ends

                halo_send[position, pl.ds(local, 16)] = lax.fori_loop(
                    0, parts, block, jnp.zeros((16, width), F32)
                )
                return carry

            lax.fori_loop(0, tall // 16, update, 0)
            halo(position, 0).start()
            halo(position, 1).start()
            if position + 2 < len(order):
                source_copy(position + 2).start()
            if final:
                if q >= 2:
                    out_copy(q - 2).wait()
            else:
                for offset in peers:
                    inward(slot, q, offset).wait_send()
            halo(position, 0).wait()
            halo(position, 1).wait()
            begin = (q % 2) * tallest * lat

            def advect(g, carry):
                c = aligned(low + g * 16)
                local = aligned(g * 16)
                stay, px, nx, py, ny = (coef[k, pl.ds(c, 16)] for k in range(5))
                both = jnp.where(
                    lane % 2 == 1,
                    pltpu.roll(halo_recv[position, 0, pl.ds(local, 16)], width - 2, 1),
                    halo_recv[position, 1, pl.ds(local, 16)],
                )

                def block(b, state_of):
                    southern, adjoint = state_of
                    ends = pltpu.roll(both, (width - 2 * b * rows) % width, 1)
                    for r in range(rows):
                        i = b * rows + r
                        northern = state[i + 1, pl.ds(c, 16)]
                        end = pltpu.roll(ends, width - 2 * r, 1) if r else ends
                        eastern = jnp.where(lane == width - 1, end, pltpu.roll(adjoint, width - 1, 1))
                        western = jnp.where(lane == 0, end, pltpu.roll(adjoint, 1, 1))
                        result = stay * adjoint + px * eastern + nx * western
                        result = result + py * northern + ny * southern
                        if final:
                            stage[pl.ds(begin + local * lat + i, 16, stride=lat)] = result
                        else:
                            emit((result + forcing[pl.ds(i, 1)]) * ocean[pl.ds(i, 1)], i, b, r, c, local)
                        southern, adjoint = adjoint, northern
                    return southern, adjoint

                lax.fori_loop(0, parts, block, (jnp.zeros((16, width), F32), state[0, pl.ds(c, 16)]))
                return carry

            lax.fori_loop(0, tall // 16, advect, 0)
            if final:
                out_copy(q).start()
            else:
                send_inward((step - 1) % 2, q, False)

    for q in range(CHUNKS):
        for offset in peers:
            inward(0, q, offset).wait_send()
            outward(q, offset).wait_send()
    if left:
        for offset in peers:
            leftover(0, offset, False).wait_send()
            leftover(1, offset, False).wait_send()
    for q in range(max(CHUNKS - 2, 0), CHUNKS):
        out_copy(q).wait()


def call(plan, identity, lam, source, mixing, drift_x, drift_y, ocean_mask, misfit, obs_mask):
    vmem = pl.BlockSpec(memory_space=pltpu.VMEM)
    smem = pl.BlockSpec(memory_space=pltpu.SMEM)
    hbm = pl.BlockSpec(memory_space=pl.ANY)
    dma = pltpu.SemaphoreType.DMA
    parts, pad, lanes, lat, width = plan.parts, plan.pad, plan.lanes, plan.lat, plan.width
    tallest = plan.tallest
    positions = plan.steps * CHUNKS
    spare = max(plan.spare, width)
    filling = (parts * spare, lanes) if plan.over else (16, width)
    unfilling = (parts * lanes, spare) if plan.over else (16, width)
    folded = max(plan.folded, 16)
    left = (parts, folded, width)
    return pl.pallas_call(
        functools.partial(kernel, plan),
        out_shape=jax.ShapeDtypeStruct((plan.own * lat, width), F32),
        in_specs=[hbm, hbm, hbm, smem, smem, vmem, vmem, vmem],
        out_specs=hbm,
        scratch_shapes=[
            pltpu.VMEM((lat + 1, pad, width), F32),
            pltpu.VMEM((parts * pad, lanes), BF16),
            pltpu.VMEM((2, parts * pad, lanes), BF16),
            pltpu.VMEM((parts * pad, lanes), BF16),
            pltpu.VMEM((parts * pad, lanes), BF16),
            pltpu.VMEM(left, BF16), pltpu.VMEM(left, BF16), pltpu.VMEM(left, BF16), pltpu.VMEM(left, BF16),
            pltpu.VMEM((parts * pad, parts * pad), BF16),
            pltpu.VMEM((round_up(parts * pad, 128), parts * plan.own), BF16),
            pltpu.VMEM((2 * tallest * lat, width), F32),
            pltpu.VMEM((2, tallest, lat, width), BF16),
            pltpu.VMEM((16 * lat, width), F32),
            pltpu.VMEM((5, pad, width), F32),
            pltpu.VMEM((lat, width), F32),
            pltpu.VMEM((lat, width), F32),
            pltpu.VMEM((lat, width), F32),
            pltpu.VMEM(filling, BF16),
            pltpu.VMEM(unfilling, BF16),
            pltpu.VMEM((parts, tallest, spare), BF16),
            pltpu.VMEM((parts, tallest, spare), F32),
            pltpu.VMEM((folded, width), F32),
            pltpu.VMEM((parts * 16, lanes), F32),
            pltpu.VMEM((16, lanes), F32),
            pltpu.VMEM((positions, tallest, width), F32),
            pltpu.VMEM((positions, 2, tallest, width), F32),
            dma((2, CHUNKS, parts)),
            dma((2, CHUNKS, parts)),
            dma((2, parts)),
            dma((2, parts)),
            dma((positions, 2)),
            dma((positions, 2)),
            dma((2,)),
            dma((2,)),
            dma,
            dma((2, CHUNKS)),
        ],
        compiler_params=pltpu.CompilerParams(
            collective_id=identity, has_side_effects=True, vmem_limit_bytes=62 * 1024 * 1024
        ),
    )(lam, source, mixing, drift_x, drift_y, ocean_mask, misfit, obs_mask)


def census_kernel(ring, parts, ocean_mask, most, mine, others, send_sem, recv_sem):
    lon = lax.axis_index("lon")
    rows = ocean_mask.shape[0] // parts
    barrier = pltpu.get_barrier_semaphore()
    for k in range(1, ring):
        pl.semaphore_signal(barrier, inc=1, device_id={"lon": lax.rem(lon + k, ring)}, device_id_type=MESH)
    worst = jnp.zeros((8, 128), F32)
    for b in range(parts):
        count = jnp.sum(ocean_mask[b * rows : (b + 1) * rows].astype(F32))
        worst = jnp.maximum(worst, jnp.full((8, 128), count, F32))
    mine[...] = worst
    pl.semaphore_wait(barrier, ring - 1)

    def copy(k, arriving):
        other = lax.rem(lon + k, ring)
        place = other if arriving else lon
        return pltpu.make_async_remote_copy(
            src_ref=mine,
            dst_ref=others.at[place],
            send_sem=send_sem.at[k],
            recv_sem=recv_sem.at[place],
            device_id={"lon": other},
            device_id_type=MESH,
        )

    for k in range(1, ring):
        copy(k, False).start()
    for k in range(1, ring):
        copy(k, True).wait_recv()
        worst = jnp.maximum(worst, others[lax.rem(lon + k, ring)])
    for k in range(1, ring):
        copy(k, False).wait_send()
    most[...] = worst


def census(ring, parts, ocean_mask):
    vmem = pl.BlockSpec(memory_space=pltpu.VMEM)
    return pl.pallas_call(
        functools.partial(census_kernel, ring, parts),
        out_shape=jax.ShapeDtypeStruct((8, 128), F32),
        in_specs=[vmem],
        out_specs=vmem,
        scratch_shapes=[
            pltpu.VMEM((8, 128), F32),
            pltpu.VMEM((ring, 8, 128), F32),
            pltpu.SemaphoreType.DMA((ring,)),
            pltpu.SemaphoreType.DMA((ring,)),
        ],
        compiler_params=pltpu.CompilerParams(collective_id=0, has_side_effects=True),
    )(ocean_mask)


def per_device(
    parts, ring, lam_final, stored_source, mixing, drift_x, drift_y, ocean_mask, misfit, obs_mask
):
    steps = stored_source.shape[0]
    own, lat, width = lam_final.shape
    rows = lat // parts
    packed = Plan(steps, parts, ring, own, lat, width, -(-rows * 13 // 16))
    whole = Plan(steps, parts, ring, own, lat, width, rows)
    most = census(ring, parts, ocean_mask)
    operands = (
        lam_final.reshape(own * lat, width), stored_source, mixing, drift_x, drift_y, ocean_mask, misfit, obs_mask
    )
    result = lax.cond(
        most[0, 0] <= packed.lanes,
        functools.partial(call, packed, 1),
        functools.partial(call, whole, 2),
        *operands,
    )
    return result.reshape(own, lat, width)


def solution(mesh):
    in_specs = (
        P("spec", None, "lon"),
        P(None, "spec", None, "lon"),
        P(),
        P(),
        P(),
        P(None, "lon"),
        P(None, None, "lon"),
        P(None, None, "lon"),
    )
    out_specs = P("spec", None, "lon")
    return jax.shard_map(
        functools.partial(per_device, mesh.shape["spec"], mesh.shape["lon"]),
        mesh=mesh, in_specs=in_specs, out_specs=out_specs, check_vma=False,
    )
```

```python
import functools

import jax
import jax.numpy as jnp
from jax import lax
from jax.experimental import pallas as pl
from jax.experimental.pallas import tpu as pltpu
from jax.sharding import PartitionSpec as P

SHARES = (4, 5, 5, 4, 3)
CHUNKS = len(SHARES)
MESH = pl.DeviceIdType.MESH
F32, BF16 = jnp.float32, jnp.bfloat16


def round_up(value, unit):
    return -(-value // unit) * unit


class Plan:
    def __init__(self, steps, parts, ring, own, lat, width, base):
        self.steps, self.parts, self.ring = steps, parts, ring
        self.own, self.lat, self.width = own, lat, width
        self.rows = lat // parts
        self.base, self.over = base, self.rows - base
        self.lanes, self.spare = base * width, (self.rows - base) * width
        self.main = own // 16 * 16
        self.left = own - self.main
        self.keeper = parts // 2
        self.pad = round_up(own, 16)
        groups = self.pad // 16
        total = sum(SHARES)
        edges = [(groups * sum(SHARES[:q]) + total // 2) // total * 16 for q in range(CHUNKS)] + [self.main]
        self.bounds = list(zip(edges[:-1], edges[1:]))
        self.folded = round_up(base * self.left, 16)

    def span(self, q):
        low, high = self.bounds[q]
        last = q == CHUNKS - 1
        held = high - low + (self.left if last else 0)
        return low, high - low, held, round_up(held, 16)

    @property
    def tallest(self):
        return max(self.span(q)[3] for q in range(CHUNKS))


def kernel(
    plan, lam, source, mixing, drift_x, drift_y, ocean_mask, misfit, obs_mask, out,
    state, sin, rin, sout, rout, sin_x, rin_x, sout_x, rout_x, sin_l, rin_l, sout_l, rout_l,
    weight_buf, mixing_buf, stage, source_buf, factor, coef, ocean, forcing, ids, shared_ids, fill, extra_in, extra_out, fold, mixed, lift,
    halo_send, halo_recv,
    send_sem, recv_sem, shared_send_sem, shared_recv_sem, left_send_sem, left_recv_sem, halo_send_sem, halo_recv_sem,
    stage_sem, source_sem, weight_sem, self_sem, shared_self_sem,
):
    me = lax.axis_index("spec")
    lon = lax.axis_index("lon")
    parts, ring, rows, lat, width = plan.parts, plan.ring, plan.rows, plan.lat, plan.width
    own, main, left, pad, lanes, base, over, spare = (
        plan.own, plan.main, plan.left, plan.pad, plan.lanes, plan.base, plan.over, plan.spare
    )
    steps, tallest = plan.steps, plan.tallest
    east, west = lax.rem(lon + 1, ring), lax.rem(lon + ring - 1, ring)
    peers = list(range(1, parts))
    order = [(step, q) for step in reversed(range(steps)) for q in range(CHUNKS)]
    lane = lax.broadcasted_iota(jnp.int32, (16, width), 1)

    def peer(offset):
        return lax.rem(me + offset, parts)

    def aligned(value):
        return pl.multiple_of(value, 16)

    def lam_copy(q):
        low, _, held, _ = plan.span(q)
        return pltpu.make_async_copy(
            lam.at[pl.ds(low * lat, held * lat)],
            stage.at[pl.ds((q % 2) * tallest * lat, held * lat)],
            stage_sem.at[q % 2],
        )

    def out_copy(q):
        low, _, held, _ = plan.span(q)
        return pltpu.make_async_copy(
            stage.at[pl.ds((q % 2) * tallest * lat, held * lat)],
            out.at[pl.ds(low * lat, held * lat)],
            stage_sem.at[q % 2],
        )

    def source_copy(position):
        step, q = order[position]
        low, _, held, _ = plan.span(q)
        return pltpu.make_async_copy(
            source.at[step, pl.ds(low, held)],
            source_buf.at[position % 2, pl.ds(0, held)],
            source_sem.at[position % 2],
        )

    mixing_copy = pltpu.make_async_copy(mixing, mixing_buf.at[pl.ds(0, parts * own)], weight_sem)

    def inward(slot, q, offset):
        low, count, _, _ = plan.span(q)
        target = peer(offset)
        return pltpu.make_async_remote_copy(
            src_ref=sin.at[pl.ds(aligned(target * pad + low), count)],
            dst_ref=rin.at[slot, pl.ds(aligned(me * pad + low), count)],
            send_sem=send_sem.at[0, q, offset],
            recv_sem=recv_sem.at[0, q, me],
            device_id={"spec": target},
            device_id_type=MESH,
        )

    def inward_arrival(slot, q, offset):
        low, count, _, _ = plan.span(q)
        origin = peer(offset)
        return pltpu.make_async_remote_copy(
            src_ref=sin.at[pl.ds(aligned(origin * pad + low), count)],
            dst_ref=rin.at[slot, pl.ds(aligned(origin * pad + low), count)],
            send_sem=send_sem.at[0, q, offset],
            recv_sem=recv_sem.at[0, q, origin],
            device_id={"spec": origin},
            device_id_type=MESH,
        )

    def inward_self(slot, q):
        low, count, _, _ = plan.span(q)
        return pltpu.make_async_copy(
            sin.at[pl.ds(aligned(me * pad + low), count)],
            rin.at[slot, pl.ds(aligned(me * pad + low), count)],
            self_sem.at[0, q],
        )

    def outward(q, offset):
        low, count, _, _ = plan.span(q)
        target = peer(offset)
        return pltpu.make_async_remote_copy(
            src_ref=sout.at[pl.ds(aligned(target * pad + low), count)],
            dst_ref=rout.at[pl.ds(aligned(me * pad + low), count)],
            send_sem=send_sem.at[1, q, offset],
            recv_sem=recv_sem.at[1, q, me],
            device_id={"spec": target},
            device_id_type=MESH,
        )

    def outward_arrival(q, offset):
        low, count, _, _ = plan.span(q)
        origin = peer(offset)
        return pltpu.make_async_remote_copy(
            src_ref=sout.at[pl.ds(aligned(origin * pad + low), count)],
            dst_ref=rout.at[pl.ds(aligned(origin * pad + low), count)],
            send_sem=send_sem.at[1, q, offset],
            recv_sem=recv_sem.at[1, q, origin],
            device_id={"spec": origin},
            device_id_type=MESH,
        )

    def outward_self(q):
        low, count, _, _ = plan.span(q)
        return pltpu.make_async_copy(
            sout.at[pl.ds(aligned(me * pad + low), count)],
            rout.at[pl.ds(aligned(me * pad + low), count)],
            self_sem.at[1, q],
        )

    keeper = plan.keeper

    def shared_in(slot, q, place):
        low, _, _, tall = plan.span(q)
        return pltpu.make_async_remote_copy(
            src_ref=sin_x.at[pl.ds(low, tall)],
            dst_ref=rin_x.at[slot, pl.ds(aligned(place * pad + low), tall)],
            send_sem=shared_send_sem.at[0, q, 0],
            recv_sem=shared_recv_sem.at[0, q, place],
            device_id={"spec": keeper},
            device_id_type=MESH,
        )

    def shared_in_self(slot, q):
        low, _, _, tall = plan.span(q)
        return pltpu.make_async_copy(
            sin_x.at[pl.ds(low, tall)],
            rin_x.at[slot, pl.ds(keeper * pad + low, tall)],
            shared_self_sem.at[0, q],
        )

    def shared_out(q, target, index):
        low, _, _, tall = plan.span(q)
        return pltpu.make_async_remote_copy(
            src_ref=sout_x.at[pl.ds(target * pad + low, tall)],
            dst_ref=rout_x.at[pl.ds(low, tall)],
            send_sem=shared_send_sem.at[1, q, index],
            recv_sem=shared_recv_sem.at[1, q, 0],
            device_id={"spec": target},
            device_id_type=MESH,
        )

    def shared_out_self(q):
        low, _, _, tall = plan.span(q)
        return pltpu.make_async_copy(
            sout_x.at[pl.ds(keeper * pad + low, tall)],
            rout_x.at[pl.ds(low, tall)],
            shared_self_sem.at[1, q],
        )

    others = [z for z in range(parts) if z != keeper]

    def leftover(phase, offset, arriving):
        sender, receiver = (sin_l, rin_l) if phase == 0 else (sout_l, rout_l)
        other = peer(offset)
        place = other if arriving else me
        return pltpu.make_async_remote_copy(
            src_ref=sender.at[other],
            dst_ref=receiver.at[place],
            send_sem=left_send_sem.at[phase, offset],
            recv_sem=left_recv_sem.at[phase, place],
            device_id={"spec": other},
            device_id_type=MESH,
        )

    def halo(position, side):
        return pltpu.make_async_remote_copy(
            src_ref=halo_send.at[position],
            dst_ref=halo_recv.at[position, side],
            send_sem=halo_send_sem.at[position, side],
            recv_sem=halo_recv_sem.at[position, side],
            device_id={"lon": west if side == 0 else east},
            device_id_type=MESH,
        )

    for q in range(min(2, CHUNKS)):
        lam_copy(q).start()
    mixing_copy.start()
    source_copy(0).start()
    source_copy(1).start()

    barrier = pltpu.get_barrier_semaphore()
    for offset in peers:
        pl.semaphore_signal(barrier, inc=1, device_id={"spec": peer(offset)}, device_id_type=MESH)
    for side in (west, east):
        pl.semaphore_signal(barrier, inc=1, device_id={"lon": side}, device_id_type=MESH)
    pl.semaphore_wait(barrier, len(peers) + 2)

    def set_forcing(step):
        forcing[...] = misfit[step] * obs_mask[step].astype(F32)

    wet = ocean_mask[...].astype(F32)
    ocean[...] = wet
    set_forcing(steps - 1)
    state[lat] = jnp.zeros((pad, width), F32)
    if left:
        lift[...] = jnp.zeros((16, lanes), F32)

    def column(numbering, row):
        return jnp.transpose(jnp.broadcast_to(numbering[pl.ds(row, 1)], (width, width)))

    def match(tall, row):
        return jnp.where(tall == ids[pl.ds(row, 1)], 1.0, 0.0).astype(BF16)

    if over:
        row_of = lax.broadcasted_iota(jnp.int32, (lat, width), 0)

        def block_of(index):
            return sum((index >= b * rows).astype(jnp.int32) for b in range(1, parts))

        riding = row_of - block_of(row_of) * rows >= base
        chosen = jnp.where(riding, wet, 1.0 - wet)
        here = lax.broadcasted_iota(jnp.int32, (lat, lat), 0)
        there = lax.broadcasted_iota(jnp.int32, (lat, lat), 1)
        block_here, block_there = block_of(here), block_of(there)
        kind_here = (here - block_here * rows >= base).astype(jnp.int32)
        kind_there = (there - block_there * rows >= base).astype(jnp.int32)
        before = (block_here == block_there) & (kind_here == kind_there) & (there < here)
        first = lax.broadcasted_iota(jnp.int32, (width, width), 0)
        second = lax.broadcasted_iota(jnp.int32, (width, width), 1)
        packed = chosen.astype(BF16)
        within = jnp.dot(packed, (first < second).astype(F32).astype(BF16), preferred_element_type=F32)
        totals = jnp.dot(packed, jnp.ones((width, width), BF16), preferred_element_type=F32)
        offset_rows = jnp.dot(
            before.astype(F32).astype(BF16), totals.astype(BF16), preferred_element_type=F32
        )
        rank = within + offset_rows
        ids[...] = jnp.where(chosen > 0.0, rank, jnp.where(riding, -1.0, -2.0))

        def count_of(kind):
            chosen_rows = ((block_here == block_there) & (kind_there == kind)).astype(F32).astype(BF16)
            return jnp.dot(chosen_rows, totals.astype(BF16), preferred_element_type=F32)

        dry = count_of(0)
        excess = jnp.maximum(count_of(1) - dry, 0.0)
        earlier = ((block_there < block_here) & (there == block_there * rows)).astype(F32).astype(BF16)
        ahead = jnp.dot(earlier, excess.astype(BF16), preferred_element_type=F32)
        shared_ids[...] = jnp.where(riding & (chosen > 0.0) & (rank >= dry), ahead + rank - dry, -1.0)
        numbers = lax.broadcasted_iota(jnp.int32, (width, width), 1).astype(F32)

        def fill_block(b, carry):
            for o in range(over):
                tall = column(ids, b * rows + base + o)
                spot = pl.ds(pl.multiple_of(b * spare + o * width, width), width)
                fill[spot, lanes:] = jnp.where(
                    column(shared_ids, b * rows + base + o) == numbers, 1.0, 0.0
                ).astype(BF16)

                def one(r, inner):
                    fill[spot, pl.ds(pl.multiple_of(r * width, width), width)] = match(tall, b * rows + r)
                    return inner

                lax.fori_loop(0, base, one, 0)
            return carry

        lax.fori_loop(0, parts, fill_block, 0)

    def emit(x, i, b, r, c, local):
        state[i, pl.ds(c, 16)] = x
        rounded = x.astype(BF16)
        if r < base:
            sin[pl.ds(aligned(b * pad + c), 16), r * width : (r + 1) * width] = rounded
        else:
            extra_in[b, pl.ds(local, 16), (r - base) * width : (r - base + 1) * width] = rounded

    def tiles(body):
        wide = lanes // (2 * width)

        def one(n, carry):
            body(pl.ds(pl.multiple_of(n * 2 * width, 2 * width), 2 * width))
            return carry

        lax.fori_loop(0, wide, one, 0)
        if wide * 2 * width < lanes:
            body(pl.ds(wide * 2 * width, width))

    def fold_rows(sender):
        def one(b, carry):
            value = sender[pl.ds(aligned(b * pad + main), 16), :].astype(F32)
            for t in range(base):
                fold[t * left : (t + 1) * left] = value[:left, t * width : (t + 1) * width]
            sin_l[b] = fold[...].astype(BF16)
            return carry

        lax.fori_loop(0, parts, one, 0)

    def send_inward(slot, q, first):
        low, count, held, tall = plan.span(q)
        last = q == CHUNKS - 1
        if over:

            def block(b, carry):
                place = pl.ds(aligned(b * pad + low), tall)

                def one(cols):
                    moved = jnp.dot(
                        extra_in[b, :tall],
                        fill[pl.ds(pl.multiple_of(b * spare, width), spare), cols],
                        preferred_element_type=F32,
                    )
                    sin[place, cols] = (sin[place, cols].astype(F32) + moved).astype(BF16)

                tiles(one)
                return carry + jnp.dot(
                    extra_in[b, :tall],
                    fill[pl.ds(pl.multiple_of(b * spare, width), spare), lanes:],
                    preferred_element_type=F32,
                )

            tile = lax.fori_loop(0, parts, block, jnp.zeros((tall, width), F32))
            if held < tall:
                tile = jnp.where(lax.broadcasted_iota(jnp.int32, (tall, width), 0) < held, tile, 0.0)
            sin_x[low : low + tall] = tile.astype(BF16)

            @pl.when(me == keeper)
            def _():
                shared_in_self(slot, q).start()

            @pl.when(me != keeper)
            def _():
                shared_in(slot, q, me).start()

        inward_self(slot, q).start()
        for offset in peers:
            inward(slot, q, offset).start()
        if last and left:
            if not first:
                for offset in peers:
                    leftover(0, offset, False).wait_send()
            fold_rows(sin)
            for offset in peers:
                leftover(0, offset, False).start()
            rin_l[me] = sin_l[me]

    for q in range(CHUNKS):
        low, count, held, tall = plan.span(q)
        lam_copy(q).wait()
        start = (q % 2) * tallest * lat

        def prepare(g, carry):
            def block(b, inner):
                for r in range(rows):
                    i = b * rows + r
                    a = stage[pl.ds(start + g * 16 * lat + i, 16, stride=lat)]
                    x = (a + forcing[pl.ds(i, 1)]) * ocean[pl.ds(i, 1)]
                    emit(x, i, b, r, aligned(low + g * 16), aligned(g * 16))
                return inner

            return lax.fori_loop(0, parts, block, carry)

        lax.fori_loop(0, tall // 16, prepare, 0)
        if q + 2 < CHUNKS:
            lam_copy(q + 2).start()
        send_inward((steps - 1) % 2, q, True)

    def coefficients(c, carry):
        speed_x = drift_x[me * own + c]
        speed_y = drift_y[me * own + c]
        values = (
            1.0 - jnp.abs(speed_x) - jnp.abs(speed_y),
            jnp.maximum(speed_x, 0.0), jnp.maximum(-speed_x, 0.0),
            jnp.maximum(speed_y, 0.0), jnp.maximum(-speed_y, 0.0),
        )
        for k, value in enumerate(values):
            coef[k, pl.ds(c, 1)] = jnp.full((1, width), value, F32)
        return carry

    lax.fori_loop(0, own, coefficients, 0)

    mixing_copy.wait()

    def arrange_weights():
        wide = mixing_buf.shape[0]
        start = 0
        pieces = [plan.bounds[q] for q in range(CHUNKS)] + ([(main, pad)] if left else [])
        for low, high in pieces:
            count = high - low
            picked = lax.broadcasted_iota(jnp.int32, (count, parts * own), 0) + low
            picking = lax.broadcasted_iota(jnp.int32, (count, parts * own), 1)
            place = lax.broadcasted_iota(jnp.int32, (count, wide), 1)

            def one(h, carry):
                pick = (picking == h * own + picked) & (picked < own)
                rows_of_home = lax.dot_general(
                    pick.astype(F32).astype(BF16), mixing_buf[...], (((1,), (1,)), ((), ())),
                    preferred_element_type=F32,
                )
                value = jnp.zeros((count, wide), F32)
                for o in range(parts):
                    shifted = pltpu.roll(rows_of_home, o * (pad - own), 1) if o and pad > own else rows_of_home
                    value = jnp.where((place >= o * pad) & (place < o * pad + own), shifted, value)
                weight_buf[pl.ds(aligned(start + h * count), count)] = value.astype(BF16)[:, : parts * pad]
                return carry

            lax.fori_loop(0, parts, one, 0)
            start += parts * count

    arrange_weights()

    for step in reversed(range(steps)):
        final = step == 0
        first = step == steps - 1
        slot = step % 2

        for q in range(CHUNKS):
            inward_self(slot, q).wait()
            for offset in peers:
                inward_arrival(slot, q, offset).wait_recv()
        if left:
            for offset in peers:
                leftover(0, offset, True).wait_recv()

            def lift_rows(o, carry):
                value = rin_l[o].astype(F32)
                for t in range(base):
                    lift[:left, t * width : (t + 1) * width] = value[t * left : (t + 1) * left]
                rin[slot, pl.ds(aligned(o * pad + main), 16)] = lift[...].astype(BF16)
                return carry

            lax.fori_loop(0, parts, lift_rows, 0)

        if over:

            @pl.when(me == keeper)
            def _():
                for q in range(CHUNKS):
                    shared_in_self(slot, q).wait()
                    for z in others:
                        shared_in(slot, q, z).wait_recv()

        start = 0
        for q in range(CHUNKS):
            low, count, held, tall = plan.span(q)
            last = q == CHUNKS - 1
            if not first:
                for offset in peers:
                    outward(q, offset).wait_send()

            def couple(cols):
                result = jnp.dot(
                    weight_buf[start : start + parts * count], rin[slot, :, cols], preferred_element_type=F32
                )
                for h in range(parts):
                    sout[h * pad + low : h * pad + low + count, cols] = result[h * count : (h + 1) * count].astype(BF16)

            tiles(couple)
            outward_self(q).start()
            for offset in peers:
                outward(q, offset).start()
            start += parts * count
            if last and left:
                if not first:
                    for offset in peers:
                        leftover(1, offset, False).wait_send()

                def couple_left(cols):
                    mixed[:, cols] = jnp.dot(
                        weight_buf[start : start + parts * 16], rin[slot, :, cols], preferred_element_type=F32
                    )

                tiles(couple_left)
                for h in range(parts):
                    for t in range(base):
                        fold[t * left : (t + 1) * left] = mixed[
                            h * 16 : h * 16 + left, t * width : (t + 1) * width
                        ]
                    sout_l[h] = fold[...].astype(BF16)
                for offset in peers:
                    leftover(1, offset, False).start()
                rout_l[me] = sout_l[me]
            if over:

                @pl.when(me == keeper)
                def _():
                    if not first:
                        for index, target in enumerate(others):
                            shared_out(q, target, index).wait_send()
                    begin = start - parts * count
                    result = jnp.dot(
                        weight_buf[begin : begin + parts * count], rin_x[slot], preferred_element_type=F32
                    ).astype(BF16)
                    for h in range(parts):
                        sout_x[h * pad + low : h * pad + low + count] = result[h * count : (h + 1) * count]
                    if last and left:
                        ends = jnp.dot(
                            weight_buf[start : start + parts * 16], rin_x[slot], preferred_element_type=F32
                        ).astype(BF16)
                        for h in range(parts):
                            sout_x[h * pad + main : h * pad + pad] = ends[h * 16 : (h + 1) * 16]
                    shared_out_self(q).start()
                    for index, target in enumerate(others):
                        shared_out(q, target, index).start()

        if not final:
            set_forcing(step - 1)
        for q in range(CHUNKS):
            low, count, held, tall = plan.span(q)
            last = q == CHUNKS - 1
            position = (steps - 1 - step) * CHUNKS + q
            source_slot = position % 2
            source_copy(position).wait()
            outward_self(q).wait()
            for offset in peers:
                outward_arrival(q, offset).wait_recv()
            if last and left:
                for offset in peers:
                    leftover(1, offset, True).wait_recv()

                def spread(b, carry):
                    value = rout_l[b].astype(F32)
                    for t in range(base):
                        lift[:left, t * width : (t + 1) * width] = value[t * left : (t + 1) * left]
                    rout[pl.ds(aligned(b * pad + main), 16)] = lift[...].astype(BF16)
                    return carry

                lax.fori_loop(0, parts, spread, 0)
            if over:

                @pl.when(me == keeper)
                def _():
                    shared_out_self(q).wait()

                @pl.when(me != keeper)
                def _():
                    shared_out(q, keeper, 0).wait_recv()

                def restore(b, carry):
                    spot = pl.ds(pl.multiple_of(b * spare, width), spare)
                    across = (((1,), (1,)), ((), ()))
                    extra_out[b, :tall] = lax.dot_general(
                        rout[pl.ds(aligned(b * pad + low), tall)], fill[spot, :lanes], across,
                        preferred_element_type=F32,
                    ) + lax.dot_general(
                        rout_x[low : low + tall], fill[spot, lanes:], across, preferred_element_type=F32
                    )
                    return carry

                lax.fori_loop(0, parts, restore, 0)

            def update(g, carry):
                c = aligned(low + g * 16)
                local = aligned(g * 16)
                for k in range(16):
                    factor[k * lat : (k + 1) * lat] = source_buf[source_slot, local + k].astype(F32)

                def block(b, edges):
                    ends = edges
                    for r in range(rows):
                        i = b * rows + r
                        if r < base:
                            coupled = rout[
                                pl.ds(aligned(b * pad + c), 16), r * width : (r + 1) * width
                            ].astype(F32)
                            if over:
                                coupled = coupled * ocean[pl.ds(i, 1)]
                        else:
                            coupled = extra_out[b, pl.ds(local, 16), (r - base) * width : (r - base + 1) * width]
                        adjoint = state[i, pl.ds(c, 16)] + factor[pl.ds(i, 16, stride=lat)] * coupled
                        state[i, pl.ds(c, 16)] = adjoint
                        place = lane - 2 * i
                        ends = jnp.where((place == 0) | (place == 1), pltpu.roll(adjoint, 2 * i + 1, 1), ends)
                    return ends

                halo_send[position, pl.ds(local, 16)] = lax.fori_loop(
                    0, parts, block, jnp.zeros((16, width), F32)
                )
                return carry

            lax.fori_loop(0, tall // 16, update, 0)
            halo(position, 0).start()
            halo(position, 1).start()
            if position + 2 < len(order):
                source_copy(position + 2).start()
            if final:
                if q >= 2:
                    out_copy(q - 2).wait()
            else:
                for offset in peers:
                    inward(slot, q, offset).wait_send()
                if over:

                    @pl.when(me != keeper)
                    def _():
                        shared_in(slot, q, me).wait_send()

            halo(position, 0).wait()
            halo(position, 1).wait()
            begin = (q % 2) * tallest * lat

            def advect(g, carry):
                c = aligned(low + g * 16)
                local = aligned(g * 16)
                stay, px, nx, py, ny = (coef[k, pl.ds(c, 16)] for k in range(5))
                both = jnp.where(
                    lane % 2 == 1,
                    pltpu.roll(halo_recv[position, 0, pl.ds(local, 16)], width - 2, 1),
                    halo_recv[position, 1, pl.ds(local, 16)],
                )

                def block(b, state_of):
                    southern, adjoint = state_of
                    ends = pltpu.roll(both, (width - 2 * b * rows) % width, 1)
                    for r in range(rows):
                        i = b * rows + r
                        northern = state[i + 1, pl.ds(c, 16)]
                        end = pltpu.roll(ends, width - 2 * r, 1) if r else ends
                        eastern = jnp.where(lane == width - 1, end, pltpu.roll(adjoint, width - 1, 1))
                        western = jnp.where(lane == 0, end, pltpu.roll(adjoint, 1, 1))
                        result = stay * adjoint + px * eastern + nx * western
                        result = result + py * northern + ny * southern
                        if final:
                            stage[pl.ds(begin + local * lat + i, 16, stride=lat)] = result
                        else:
                            emit((result + forcing[pl.ds(i, 1)]) * ocean[pl.ds(i, 1)], i, b, r, c, local)
                        southern, adjoint = adjoint, northern
                    return southern, adjoint

                lax.fori_loop(0, parts, block, (jnp.zeros((16, width), F32), state[0, pl.ds(c, 16)]))
                return carry

            lax.fori_loop(0, tall // 16, advect, 0)
            if final:
                out_copy(q).start()
            else:
                send_inward((step - 1) % 2, q, False)

    for q in range(CHUNKS):
        for offset in peers:
            inward(0, q, offset).wait_send()
            outward(q, offset).wait_send()
        if over:

            @pl.when(me == keeper)
            def _():
                for index, target in enumerate(others):
                    shared_out(q, target, index).wait_send()

            @pl.when(me != keeper)
            def _():
                shared_in(0, q, me).wait_send()

    if left:
        for offset in peers:
            leftover(0, offset, False).wait_send()
            leftover(1, offset, False).wait_send()
    for q in range(max(CHUNKS - 2, 0), CHUNKS):
        out_copy(q).wait()


def call(plan, identity, lam, source, mixing, drift_x, drift_y, ocean_mask, misfit, obs_mask):
    vmem = pl.BlockSpec(memory_space=pltpu.VMEM)
    smem = pl.BlockSpec(memory_space=pltpu.SMEM)
    hbm = pl.BlockSpec(memory_space=pl.ANY)
    dma = pltpu.SemaphoreType.DMA
    parts, pad, lanes, lat, width = plan.parts, plan.pad, plan.lanes, plan.lat, plan.width
    tallest = plan.tallest
    positions = plan.steps * CHUNKS
    spare = max(plan.spare, width)
    filling = (parts * spare, lanes + width) if plan.over else (16, width)
    tile = (pad, width) if plan.over else (16, width)
    gathered = (parts * pad, width) if plan.over else (16, width)
    folded = max(plan.folded, 16)
    left = (parts, folded, width)
    return pl.pallas_call(
        functools.partial(kernel, plan),
        out_shape=jax.ShapeDtypeStruct((plan.own * lat, width), F32),
        in_specs=[hbm, hbm, hbm, smem, smem, vmem, vmem, vmem],
        out_specs=hbm,
        scratch_shapes=[
            pltpu.VMEM((lat + 1, pad, width), F32),
            pltpu.VMEM((parts * pad, lanes), BF16),
            pltpu.VMEM((2, parts * pad, lanes), BF16),
            pltpu.VMEM((parts * pad, lanes), BF16),
            pltpu.VMEM((parts * pad, lanes), BF16),
            pltpu.VMEM(tile, BF16), pltpu.VMEM((2,) + gathered, BF16), pltpu.VMEM(gathered, BF16), pltpu.VMEM(tile, BF16),
            pltpu.VMEM(left, BF16), pltpu.VMEM(left, BF16), pltpu.VMEM(left, BF16), pltpu.VMEM(left, BF16),
            pltpu.VMEM((parts * pad, parts * pad), BF16),
            pltpu.VMEM((round_up(parts * pad, 128), parts * plan.own), BF16),
            pltpu.VMEM((2 * tallest * lat, width), F32),
            pltpu.VMEM((2, tallest, lat, width), BF16),
            pltpu.VMEM((16 * lat, width), F32),
            pltpu.VMEM((5, pad, width), F32),
            pltpu.VMEM((lat, width), F32),
            pltpu.VMEM((lat, width), F32),
            pltpu.VMEM((lat, width), F32),
            pltpu.VMEM((lat, width), F32),
            pltpu.VMEM(filling, BF16),
            pltpu.VMEM((parts, tallest, spare), BF16),
            pltpu.VMEM((parts, tallest, spare), F32),
            pltpu.VMEM((folded, width), F32),
            pltpu.VMEM((parts * 16, lanes), F32),
            pltpu.VMEM((16, lanes), F32),
            pltpu.VMEM((positions, tallest, width), F32),
            pltpu.VMEM((positions, 2, tallest, width), F32),
            dma((2, CHUNKS, parts)),
            dma((2, CHUNKS, parts)),
            dma((2, CHUNKS, parts)),
            dma((2, CHUNKS, parts)),
            dma((2, parts)),
            dma((2, parts)),
            dma((positions, 2)),
            dma((positions, 2)),
            dma((2,)),
            dma((2,)),
            dma,
            dma((2, CHUNKS)),
            dma((2, CHUNKS)),
        ],
        compiler_params=pltpu.CompilerParams(
            collective_id=identity, has_side_effects=True, vmem_limit_bytes=62 * 1024 * 1024
        ),
    )(lam, source, mixing, drift_x, drift_y, ocean_mask, misfit, obs_mask)


def census_kernel(ring, plan, ocean_mask, most, mine, others, send_sem, recv_sem):
    lon = lax.axis_index("lon")
    rows = plan.rows
    barrier = pltpu.get_barrier_semaphore()
    for k in range(1, ring):
        pl.semaphore_signal(barrier, inc=1, device_id={"lon": lax.rem(lon + k, ring)}, device_id_type=MESH)
    worst = jnp.zeros((8, 128), F32)
    for b in range(plan.parts):
        count = jnp.sum(ocean_mask[b * rows : (b + 1) * rows].astype(F32))
        worst = worst + jnp.full((8, 128), jnp.maximum(count - plan.lanes, 0.0), F32)
    mine[...] = worst
    pl.semaphore_wait(barrier, ring - 1)

    def copy(k, arriving):
        other = lax.rem(lon + k, ring)
        place = other if arriving else lon
        return pltpu.make_async_remote_copy(
            src_ref=mine,
            dst_ref=others.at[place],
            send_sem=send_sem.at[k],
            recv_sem=recv_sem.at[place],
            device_id={"lon": other},
            device_id_type=MESH,
        )

    for k in range(1, ring):
        copy(k, False).start()
    for k in range(1, ring):
        copy(k, True).wait_recv()
        worst = jnp.maximum(worst, others[lax.rem(lon + k, ring)])
    for k in range(1, ring):
        copy(k, False).wait_send()
    most[...] = worst


def census(ring, plan, ocean_mask):
    vmem = pl.BlockSpec(memory_space=pltpu.VMEM)
    return pl.pallas_call(
        functools.partial(census_kernel, ring, plan),
        out_shape=jax.ShapeDtypeStruct((8, 128), F32),
        in_specs=[vmem],
        out_specs=vmem,
        scratch_shapes=[
            pltpu.VMEM((8, 128), F32),
            pltpu.VMEM((ring, 8, 128), F32),
            pltpu.SemaphoreType.DMA((ring,)),
            pltpu.SemaphoreType.DMA((ring,)),
        ],
        compiler_params=pltpu.CompilerParams(collective_id=0, has_side_effects=True),
    )(ocean_mask)


def per_device(
    parts, ring, lam_final, stored_source, mixing, drift_x, drift_y, ocean_mask, misfit, obs_mask
):
    steps = stored_source.shape[0]
    own, lat, width = lam_final.shape
    rows = lat // parts
    packed = Plan(steps, parts, ring, own, lat, width, rows * 3 // 4)
    whole = Plan(steps, parts, ring, own, lat, width, rows)
    most = census(ring, packed, ocean_mask)
    operands = (
        lam_final.reshape(own * lat, width), stored_source, mixing, drift_x, drift_y, ocean_mask, misfit, obs_mask
    )
    result = lax.cond(
        most[0, 0] <= width,
        functools.partial(call, packed, 1),
        functools.partial(call, whole, 2),
        *operands,
    )
    return result.reshape(own, lat, width)


def solution(mesh):
    in_specs = (
        P("spec", None, "lon"),
        P(None, "spec", None, "lon"),
        P(),
        P(),
        P(),
        P(None, "lon"),
        P(None, None, "lon"),
        P(None, None, "lon"),
    )
    out_specs = P("spec", None, "lon")
    return jax.shard_map(
        functools.partial(per_device, mesh.shape["spec"], mesh.shape["lon"]),
        mesh=mesh, in_specs=in_specs, out_specs=out_specs, check_vma=False,
    )
```

```python
import functools

import jax
import jax.numpy as jnp
from jax import lax
from jax.experimental import pallas as pl
from jax.experimental.pallas import tpu as pltpu
from jax.sharding import PartitionSpec as P

SHARES = (3, 5, 5, 5, 3)
CHUNKS = len(SHARES)
MESH = pl.DeviceIdType.MESH
F32, BF16 = jnp.float32, jnp.bfloat16


def round_up(value, unit):
    return -(-value // unit) * unit


class Plan:
    def __init__(self, steps, parts, ring, own, lat, width, base):
        self.steps, self.parts, self.ring = steps, parts, ring
        self.own, self.lat, self.width = own, lat, width
        self.rows = lat // parts
        self.base, self.over = base, self.rows - base
        self.lanes, self.spare = base * width, (self.rows - base) * width
        self.main = own // 16 * 16
        self.left = own - self.main
        self.keeper = parts // 2
        self.pad = round_up(own, 16)
        groups = self.pad // 16
        total = sum(SHARES)
        edges = [(groups * sum(SHARES[1:q]) + total // 2) // total * 16 for q in range(1, CHUNKS + 1)] + [self.main]
        self.bounds = [(edges[-2], edges[-1])] + list(zip(edges[:-2], edges[1:-1]))
        self.folded = round_up(base * self.left, 16)

    def span(self, q):
        low, high = self.bounds[q]
        held = high - low + (self.left if q == 0 else 0)
        return low, high - low, held, round_up(held, 16)

    @property
    def tallest(self):
        return max(self.span(q)[3] for q in range(CHUNKS))


def kernel(
    plan, lam, source, mixing, drift_x, drift_y, ocean_mask, misfit, obs_mask, out,
    state, sin, rin, sout, rout, sin_x, rin_x, sout_x, rout_x, sin_l, rin_l, sout_l, rout_l,
    weight_buf, mixing_buf, stage, source_buf, factor, coef, ocean, forcing, ids, shared_ids, fill, extra_in, extra_out, fold, mixed, lift,
    halo_send, halo_recv,
    send_sem, recv_sem, shared_send_sem, shared_recv_sem, left_send_sem, left_recv_sem, halo_send_sem, halo_recv_sem,
    stage_sem, source_sem, weight_sem, self_sem, shared_self_sem,
):
    me = lax.axis_index("spec")
    lon = lax.axis_index("lon")
    parts, ring, rows, lat, width = plan.parts, plan.ring, plan.rows, plan.lat, plan.width
    own, main, left, pad, lanes, base, over, spare = (
        plan.own, plan.main, plan.left, plan.pad, plan.lanes, plan.base, plan.over, plan.spare
    )
    steps, tallest = plan.steps, plan.tallest
    east, west = lax.rem(lon + 1, ring), lax.rem(lon + ring - 1, ring)
    peers = list(range(1, parts))
    order = [(step, q) for step in reversed(range(steps)) for q in range(CHUNKS)]
    lane = lax.broadcasted_iota(jnp.int32, (16, width), 1)

    def peer(offset):
        return lax.rem(me + offset, parts)

    def aligned(value):
        return pl.multiple_of(value, 16)

    def lam_copy(q):
        low, _, held, _ = plan.span(q)
        return pltpu.make_async_copy(
            lam.at[pl.ds(low * lat, held * lat)],
            stage.at[pl.ds((q % 2) * tallest * lat, held * lat)],
            stage_sem.at[q % 2],
        )

    def out_copy(q):
        low, _, held, _ = plan.span(q)
        return pltpu.make_async_copy(
            stage.at[pl.ds((q % 2) * tallest * lat, held * lat)],
            out.at[pl.ds(low * lat, held * lat)],
            stage_sem.at[q % 2],
        )

    def source_copy(position):
        step, q = order[position]
        low, _, held, _ = plan.span(q)
        return pltpu.make_async_copy(
            source.at[step, pl.ds(low, held)],
            source_buf.at[position % 2, pl.ds(0, held)],
            source_sem.at[position % 2],
        )

    mixing_copy = pltpu.make_async_copy(mixing, mixing_buf.at[pl.ds(0, parts * own)], weight_sem)

    def inward(slot, q, offset):
        low, count, _, _ = plan.span(q)
        target = peer(offset)
        return pltpu.make_async_remote_copy(
            src_ref=sin.at[pl.ds(aligned(target * pad + low), count)],
            dst_ref=rin.at[slot, pl.ds(aligned(me * pad + low), count)],
            send_sem=send_sem.at[0, q, offset],
            recv_sem=recv_sem.at[0, q, me],
            device_id={"spec": target},
            device_id_type=MESH,
        )

    def inward_arrival(slot, q, offset):
        low, count, _, _ = plan.span(q)
        origin = peer(offset)
        return pltpu.make_async_remote_copy(
            src_ref=sin.at[pl.ds(aligned(origin * pad + low), count)],
            dst_ref=rin.at[slot, pl.ds(aligned(origin * pad + low), count)],
            send_sem=send_sem.at[0, q, offset],
            recv_sem=recv_sem.at[0, q, origin],
            device_id={"spec": origin},
            device_id_type=MESH,
        )

    def inward_self(slot, q):
        low, count, _, _ = plan.span(q)
        return pltpu.make_async_copy(
            sin.at[pl.ds(aligned(me * pad + low), count)],
            rin.at[slot, pl.ds(aligned(me * pad + low), count)],
            self_sem.at[0, q],
        )

    def outward(q, offset):
        low, count, _, _ = plan.span(q)
        target = peer(offset)
        return pltpu.make_async_remote_copy(
            src_ref=sout.at[pl.ds(aligned(target * pad + low), count)],
            dst_ref=rout.at[pl.ds(aligned(me * pad + low), count)],
            send_sem=send_sem.at[1, q, offset],
            recv_sem=recv_sem.at[1, q, me],
            device_id={"spec": target},
            device_id_type=MESH,
        )

    def outward_arrival(q, offset):
        low, count, _, _ = plan.span(q)
        origin = peer(offset)
        return pltpu.make_async_remote_copy(
            src_ref=sout.at[pl.ds(aligned(origin * pad + low), count)],
            dst_ref=rout.at[pl.ds(aligned(origin * pad + low), count)],
            send_sem=send_sem.at[1, q, offset],
            recv_sem=recv_sem.at[1, q, origin],
            device_id={"spec": origin},
            device_id_type=MESH,
        )

    def outward_self(q):
        low, count, _, _ = plan.span(q)
        return pltpu.make_async_copy(
            sout.at[pl.ds(aligned(me * pad + low), count)],
            rout.at[pl.ds(aligned(me * pad + low), count)],
            self_sem.at[1, q],
        )

    keeper = plan.keeper

    def shared_in(slot, q, place):
        low, _, _, tall = plan.span(q)
        return pltpu.make_async_remote_copy(
            src_ref=sin_x.at[pl.ds(low, tall)],
            dst_ref=rin_x.at[slot, pl.ds(aligned(place * pad + low), tall)],
            send_sem=shared_send_sem.at[0, q, 0],
            recv_sem=shared_recv_sem.at[0, q, place],
            device_id={"spec": keeper},
            device_id_type=MESH,
        )

    def shared_in_self(slot, q):
        low, _, _, tall = plan.span(q)
        return pltpu.make_async_copy(
            sin_x.at[pl.ds(low, tall)],
            rin_x.at[slot, pl.ds(keeper * pad + low, tall)],
            shared_self_sem.at[0, q],
        )

    def shared_out(q, target, index):
        low, _, _, tall = plan.span(q)
        return pltpu.make_async_remote_copy(
            src_ref=sout_x.at[pl.ds(target * pad + low, tall)],
            dst_ref=rout_x.at[pl.ds(low, tall)],
            send_sem=shared_send_sem.at[1, q, index],
            recv_sem=shared_recv_sem.at[1, q, 0],
            device_id={"spec": target},
            device_id_type=MESH,
        )

    def shared_out_self(q):
        low, _, _, tall = plan.span(q)
        return pltpu.make_async_copy(
            sout_x.at[pl.ds(keeper * pad + low, tall)],
            rout_x.at[pl.ds(low, tall)],
            shared_self_sem.at[1, q],
        )

    others = [z for z in range(parts) if z != keeper]

    def leftover(phase, offset, arriving):
        sender, receiver = (sin_l, rin_l) if phase == 0 else (sout_l, rout_l)
        other = peer(offset)
        place = other if arriving else me
        return pltpu.make_async_remote_copy(
            src_ref=sender.at[other],
            dst_ref=receiver.at[place],
            send_sem=left_send_sem.at[phase, offset],
            recv_sem=left_recv_sem.at[phase, place],
            device_id={"spec": other},
            device_id_type=MESH,
        )

    def halo(position, side):
        return pltpu.make_async_remote_copy(
            src_ref=halo_send.at[position],
            dst_ref=halo_recv.at[position, side],
            send_sem=halo_send_sem.at[position, side],
            recv_sem=halo_recv_sem.at[position, side],
            device_id={"lon": west if side == 0 else east},
            device_id_type=MESH,
        )

    for q in range(min(2, CHUNKS)):
        lam_copy(q).start()
    mixing_copy.start()
    source_copy(0).start()
    source_copy(1).start()

    barrier = pltpu.get_barrier_semaphore()
    for offset in peers:
        pl.semaphore_signal(barrier, inc=1, device_id={"spec": peer(offset)}, device_id_type=MESH)
    for side in (west, east):
        pl.semaphore_signal(barrier, inc=1, device_id={"lon": side}, device_id_type=MESH)
    pl.semaphore_wait(barrier, len(peers) + 2)

    def set_forcing(step):
        forcing[...] = misfit[step] * obs_mask[step].astype(F32)

    wet = ocean_mask[...].astype(F32)
    ocean[...] = wet
    set_forcing(steps - 1)
    state[lat] = jnp.zeros((pad, width), F32)
    if left:
        lift[...] = jnp.zeros((16, lanes), F32)

    def column(numbering, row):
        return jnp.transpose(jnp.broadcast_to(numbering[pl.ds(row, 1)], (width, width)))

    def match(tall, row):
        return jnp.where(tall == ids[pl.ds(row, 1)], 1.0, 0.0).astype(BF16)

    if over:
        row_of = lax.broadcasted_iota(jnp.int32, (lat, width), 0)

        def block_of(index):
            return sum((index >= b * rows).astype(jnp.int32) for b in range(1, parts))

        riding = row_of - block_of(row_of) * rows >= base
        chosen = jnp.where(riding, wet, 1.0 - wet)
        here = lax.broadcasted_iota(jnp.int32, (lat, lat), 0)
        there = lax.broadcasted_iota(jnp.int32, (lat, lat), 1)
        block_here, block_there = block_of(here), block_of(there)
        kind_here = (here - block_here * rows >= base).astype(jnp.int32)
        kind_there = (there - block_there * rows >= base).astype(jnp.int32)
        before = (block_here == block_there) & (kind_here == kind_there) & (there < here)
        first = lax.broadcasted_iota(jnp.int32, (width, width), 0)
        second = lax.broadcasted_iota(jnp.int32, (width, width), 1)
        packed = chosen.astype(BF16)
        within = jnp.dot(packed, (first < second).astype(F32).astype(BF16), preferred_element_type=F32)
        totals = jnp.dot(packed, jnp.ones((width, width), BF16), preferred_element_type=F32)
        offset_rows = jnp.dot(
            before.astype(F32).astype(BF16), totals.astype(BF16), preferred_element_type=F32
        )
        rank = within + offset_rows
        ids[...] = jnp.where(chosen > 0.0, rank, jnp.where(riding, -1.0, -2.0))

        def count_of(kind):
            chosen_rows = ((block_here == block_there) & (kind_there == kind)).astype(F32).astype(BF16)
            return jnp.dot(chosen_rows, totals.astype(BF16), preferred_element_type=F32)

        dry = count_of(0)
        excess = jnp.maximum(count_of(1) - dry, 0.0)
        earlier = ((block_there < block_here) & (there == block_there * rows)).astype(F32).astype(BF16)
        ahead = jnp.dot(earlier, excess.astype(BF16), preferred_element_type=F32)
        shared_ids[...] = jnp.where(riding & (chosen > 0.0) & (rank >= dry), ahead + rank - dry, -1.0)
        numbers = lax.broadcasted_iota(jnp.int32, (width, width), 1).astype(F32)

        def fill_block(b, carry):
            for o in range(over):
                tall = column(ids, b * rows + base + o)
                spot = pl.ds(pl.multiple_of(b * spare + o * width, width), width)
                fill[spot, lanes:] = jnp.where(
                    column(shared_ids, b * rows + base + o) == numbers, 1.0, 0.0
                ).astype(BF16)

                def one(r, inner):
                    fill[spot, pl.ds(pl.multiple_of(r * width, width), width)] = match(tall, b * rows + r)
                    return inner

                lax.fori_loop(0, base, one, 0)
            return carry


    def emit(x, i, b, r, c, local):
        state[i, pl.ds(c, 16)] = x
        rounded = x.astype(BF16)
        if r < base:
            sin[pl.ds(aligned(b * pad + c), 16), r * width : (r + 1) * width] = rounded
        else:
            extra_in[b, pl.ds(local, 16), (r - base) * width : (r - base + 1) * width] = rounded

    def tiles(body):
        wide = lanes // (2 * width)

        def one(n, carry):
            body(pl.ds(pl.multiple_of(n * 2 * width, 2 * width), 2 * width))
            return carry

        lax.fori_loop(0, wide, one, 0)
        if wide * 2 * width < lanes:
            body(pl.ds(wide * 2 * width, width))

    def fold_rows(sender):
        def one(b, carry):
            value = sender[pl.ds(aligned(b * pad + main), 16), :].astype(F32)
            for t in range(base):
                fold[t * left : (t + 1) * left] = value[:left, t * width : (t + 1) * width]
            sin_l[b] = fold[...].astype(BF16)
            return carry

        lax.fori_loop(0, parts, one, 0)

    def send_inward(slot, q, first):
        low, count, held, tall = plan.span(q)
        ends = q == 0
        if over:

            def block(turn, carry):
                offset = parts - 1 - turn
                b = peer(offset)
                if first and q == 0:
                    fill_block(b, 0)
                place = pl.ds(aligned(b * pad + low), tall)

                def one(cols):
                    moved = jnp.dot(
                        extra_in[b, :tall],
                        fill[pl.ds(pl.multiple_of(b * spare, width), spare), cols],
                        preferred_element_type=F32,
                    )
                    sin[place, cols] = (sin[place, cols].astype(F32) + moved).astype(BF16)

                tiles(one)

                @pl.when(offset > 0)
                def _():
                    inward(slot, q, offset).start()

                return carry + jnp.dot(
                    extra_in[b, :tall],
                    fill[pl.ds(pl.multiple_of(b * spare, width), spare), lanes:],
                    preferred_element_type=F32,
                )

            tile = lax.fori_loop(0, parts, block, jnp.zeros((tall, width), F32))
            if held < tall:
                tile = jnp.where(lax.broadcasted_iota(jnp.int32, (tall, width), 0) < held, tile, 0.0)
            sin_x[low : low + tall] = tile.astype(BF16)

            @pl.when(me == keeper)
            def _():
                shared_in_self(slot, q).start()

            @pl.when(me != keeper)
            def _():
                shared_in(slot, q, me).start()

        else:
            for offset in peers:
                inward(slot, q, offset).start()
        inward_self(slot, q).start()
        if ends and left:
            if not first:
                for offset in peers:
                    leftover(0, offset, False).wait_send()
            fold_rows(sin)
            for offset in peers:
                leftover(0, offset, False).start()
            rin_l[me] = sin_l[me]

    for q in range(CHUNKS):
        low, count, held, tall = plan.span(q)
        lam_copy(q).wait()
        start = (q % 2) * tallest * lat

        def prepare(g, carry):
            def block(b, inner):
                for r in range(rows):
                    i = b * rows + r
                    a = stage[pl.ds(start + g * 16 * lat + i, 16, stride=lat)]
                    x = (a + forcing[pl.ds(i, 1)]) * ocean[pl.ds(i, 1)]
                    emit(x, i, b, r, aligned(low + g * 16), aligned(g * 16))
                return inner

            return lax.fori_loop(0, parts, block, carry)

        lax.fori_loop(0, tall // 16, prepare, 0)
        if q + 2 < CHUNKS:
            lam_copy(q + 2).start()
        send_inward((steps - 1) % 2, q, True)

    def coefficients(c, carry):
        speed_x = drift_x[me * own + c]
        speed_y = drift_y[me * own + c]
        values = (
            1.0 - jnp.abs(speed_x) - jnp.abs(speed_y),
            jnp.maximum(speed_x, 0.0), jnp.maximum(-speed_x, 0.0),
            jnp.maximum(speed_y, 0.0), jnp.maximum(-speed_y, 0.0),
        )
        for k, value in enumerate(values):
            coef[k, pl.ds(c, 1)] = jnp.full((1, width), value, F32)
        return carry

    lax.fori_loop(0, own, coefficients, 0)

    mixing_copy.wait()

    def arrange_weights():
        wide = mixing_buf.shape[0]
        start = 0
        pieces = [plan.bounds[q] for q in range(CHUNKS)] + ([(main, pad)] if left else [])
        for low, high in pieces:
            count = high - low
            picked = lax.broadcasted_iota(jnp.int32, (count, parts * own), 0) + low
            picking = lax.broadcasted_iota(jnp.int32, (count, parts * own), 1)
            place = lax.broadcasted_iota(jnp.int32, (count, wide), 1)

            def one(h, carry):
                pick = (picking == h * own + picked) & (picked < own)
                rows_of_home = lax.dot_general(
                    pick.astype(F32).astype(BF16), mixing_buf[...], (((1,), (1,)), ((), ())),
                    preferred_element_type=F32,
                )
                value = jnp.zeros((count, wide), F32)
                for o in range(parts):
                    shifted = pltpu.roll(rows_of_home, o * (pad - own), 1) if o and pad > own else rows_of_home
                    value = jnp.where((place >= o * pad) & (place < o * pad + own), shifted, value)
                weight_buf[pl.ds(aligned(start + h * count), count)] = value.astype(BF16)[:, : parts * pad]
                return carry

            lax.fori_loop(0, parts, one, 0)
            start += parts * count

    arrange_weights()

    for step in reversed(range(steps)):
        final = step == 0
        first = step == steps - 1
        slot = step % 2

        if left:
            for offset in peers:
                leftover(0, offset, True).wait_recv()

            def lift_rows(o, carry):
                value = rin_l[o].astype(F32)
                for t in range(base):
                    lift[:left, t * width : (t + 1) * width] = value[t * left : (t + 1) * left]
                rin[slot, pl.ds(aligned(o * pad + main), 16)] = lift[...].astype(BF16)
                return carry

            lax.fori_loop(0, parts, lift_rows, 0)

        for q in range(CHUNKS):
            inward_self(slot, q).wait()
            for offset in peers:
                inward_arrival(slot, q, offset).wait_recv()
        if over:

            @pl.when(me == keeper)
            def _():
                for q in range(CHUNKS):
                    shared_in_self(slot, q).wait()
                    for z in others:
                        shared_in(slot, q, z).wait_recv()

        start = 0
        for q in range(CHUNKS):
            low, count, held, tall = plan.span(q)
            ends = q == 0
            if not first:
                for offset in peers:
                    outward(q, offset).wait_send()

            def couple(cols):
                result = jnp.dot(
                    weight_buf[start : start + parts * count], rin[slot, :, cols], preferred_element_type=F32
                )
                for h in range(parts):
                    sout[h * pad + low : h * pad + low + count, cols] = result[h * count : (h + 1) * count].astype(BF16)

            tiles(couple)
            outward_self(q).start()
            for offset in peers:
                outward(q, offset).start()
            start += parts * count
            if ends and left:
                if not first:
                    for offset in peers:
                        leftover(1, offset, False).wait_send()

                def couple_left(cols):
                    mixed[:, cols] = jnp.dot(
                        weight_buf[parts * main :], rin[slot, :, cols], preferred_element_type=F32
                    )

                tiles(couple_left)
                for h in range(parts):
                    for t in range(base):
                        fold[t * left : (t + 1) * left] = mixed[
                            h * 16 : h * 16 + left, t * width : (t + 1) * width
                        ]
                    sout_l[h] = fold[...].astype(BF16)
                for offset in peers:
                    leftover(1, offset, False).start()
                rout_l[me] = sout_l[me]
            if over:

                @pl.when(me == keeper)
                def _():
                    if not first:
                        for index, target in enumerate(others):
                            shared_out(q, target, index).wait_send()
                    begin = start - parts * count
                    result = jnp.dot(
                        weight_buf[begin : begin + parts * count], rin_x[slot], preferred_element_type=F32
                    ).astype(BF16)
                    for h in range(parts):
                        sout_x[h * pad + low : h * pad + low + count] = result[h * count : (h + 1) * count]
                    if ends and left:
                        tail = jnp.dot(
                            weight_buf[parts * main :], rin_x[slot], preferred_element_type=F32
                        ).astype(BF16)
                        for h in range(parts):
                            sout_x[h * pad + main : h * pad + pad] = tail[h * 16 : (h + 1) * 16]
                    shared_out_self(q).start()
                    for index, target in enumerate(others):
                        shared_out(q, target, index).start()

        if not final:
            set_forcing(step - 1)
        for q in range(CHUNKS):
            low, count, held, tall = plan.span(q)
            ends = q == 0
            position = (steps - 1 - step) * CHUNKS + q
            source_slot = position % 2
            source_copy(position).wait()
            outward_self(q).wait()
            for offset in peers:
                outward_arrival(q, offset).wait_recv()
            if ends and left:
                for offset in peers:
                    leftover(1, offset, True).wait_recv()

                def spread(b, carry):
                    value = rout_l[b].astype(F32)
                    for t in range(base):
                        lift[:left, t * width : (t + 1) * width] = value[t * left : (t + 1) * left]
                    rout[pl.ds(aligned(b * pad + main), 16)] = lift[...].astype(BF16)
                    return carry

                lax.fori_loop(0, parts, spread, 0)
            if over:

                @pl.when(me == keeper)
                def _():
                    shared_out_self(q).wait()

                @pl.when(me != keeper)
                def _():
                    shared_out(q, keeper, 0).wait_recv()

                def restore(b, carry):
                    spot = pl.ds(pl.multiple_of(b * spare, width), spare)
                    across = (((1,), (1,)), ((), ()))
                    extra_out[b, :tall] = lax.dot_general(
                        rout[pl.ds(aligned(b * pad + low), tall)], fill[spot, :lanes], across,
                        preferred_element_type=F32,
                    ) + lax.dot_general(
                        rout_x[low : low + tall], fill[spot, lanes:], across, preferred_element_type=F32
                    )
                    return carry

                lax.fori_loop(0, parts, restore, 0)

            def update(g, carry):
                c = aligned(low + g * 16)
                local = aligned(g * 16)
                for k in range(16):
                    factor[k * lat : (k + 1) * lat] = source_buf[source_slot, local + k].astype(F32)

                def block(b, edges):
                    tips = edges
                    for r in range(rows):
                        i = b * rows + r
                        if r < base:
                            coupled = rout[
                                pl.ds(aligned(b * pad + c), 16), r * width : (r + 1) * width
                            ].astype(F32)
                            if over:
                                coupled = coupled * ocean[pl.ds(i, 1)]
                        else:
                            coupled = extra_out[b, pl.ds(local, 16), (r - base) * width : (r - base + 1) * width]
                        adjoint = state[i, pl.ds(c, 16)] + factor[pl.ds(i, 16, stride=lat)] * coupled
                        state[i, pl.ds(c, 16)] = adjoint
                        place = lane - 2 * i
                        tips = jnp.where((place == 0) | (place == 1), pltpu.roll(adjoint, 2 * i + 1, 1), tips)
                    return tips

                halo_send[position, pl.ds(local, 16)] = lax.fori_loop(
                    0, parts, block, jnp.zeros((16, width), F32)
                )
                return carry

            lax.fori_loop(0, tall // 16, update, 0)
            halo(position, 0).start()
            halo(position, 1).start()
            if position + 2 < len(order):
                source_copy(position + 2).start()
            if final:
                if q >= 2:
                    out_copy(q - 2).wait()
            else:
                for offset in peers:
                    inward(slot, q, offset).wait_send()
                if over:

                    @pl.when(me != keeper)
                    def _():
                        shared_in(slot, q, me).wait_send()

            halo(position, 0).wait()
            halo(position, 1).wait()
            begin = (q % 2) * tallest * lat

            def advect(g, carry):
                c = aligned(low + g * 16)
                local = aligned(g * 16)
                stay, px, nx, py, ny = (coef[k, pl.ds(c, 16)] for k in range(5))
                both = jnp.where(
                    lane % 2 == 1,
                    pltpu.roll(halo_recv[position, 0, pl.ds(local, 16)], width - 2, 1),
                    halo_recv[position, 1, pl.ds(local, 16)],
                )

                def block(b, state_of):
                    southern, adjoint = state_of
                    tips = pltpu.roll(both, (width - 2 * b * rows) % width, 1)
                    for r in range(rows):
                        i = b * rows + r
                        northern = state[i + 1, pl.ds(c, 16)]
                        tip = pltpu.roll(tips, width - 2 * r, 1) if r else tips
                        eastern = jnp.where(lane == width - 1, tip, pltpu.roll(adjoint, width - 1, 1))
                        western = jnp.where(lane == 0, tip, pltpu.roll(adjoint, 1, 1))
                        result = stay * adjoint + px * eastern + nx * western
                        result = result + py * northern + ny * southern
                        if final:
                            stage[pl.ds(begin + local * lat + i, 16, stride=lat)] = result
                        else:
                            emit((result + forcing[pl.ds(i, 1)]) * ocean[pl.ds(i, 1)], i, b, r, c, local)
                        southern, adjoint = adjoint, northern
                    return southern, adjoint

                lax.fori_loop(0, parts, block, (jnp.zeros((16, width), F32), state[0, pl.ds(c, 16)]))
                return carry

            lax.fori_loop(0, tall // 16, advect, 0)
            if final:
                out_copy(q).start()
            else:
                send_inward((step - 1) % 2, q, False)

    for q in range(CHUNKS):
        for offset in peers:
            inward(0, q, offset).wait_send()
            outward(q, offset).wait_send()
        if over:

            @pl.when(me == keeper)
            def _():
                for index, target in enumerate(others):
                    shared_out(q, target, index).wait_send()

            @pl.when(me != keeper)
            def _():
                shared_in(0, q, me).wait_send()

    if left:
        for offset in peers:
            leftover(0, offset, False).wait_send()
            leftover(1, offset, False).wait_send()
    for q in range(max(CHUNKS - 2, 0), CHUNKS):
        out_copy(q).wait()


def call(plan, identity, lam, source, mixing, drift_x, drift_y, ocean_mask, misfit, obs_mask):
    vmem = pl.BlockSpec(memory_space=pltpu.VMEM)
    smem = pl.BlockSpec(memory_space=pltpu.SMEM)
    hbm = pl.BlockSpec(memory_space=pl.ANY)
    dma = pltpu.SemaphoreType.DMA
    parts, pad, lanes, lat, width = plan.parts, plan.pad, plan.lanes, plan.lat, plan.width
    tallest = plan.tallest
    positions = plan.steps * CHUNKS
    spare = max(plan.spare, width)
    filling = (parts * spare, lanes + width) if plan.over else (16, width)
    tile = (pad, width) if plan.over else (16, width)
    gathered = (parts * pad, width) if plan.over else (16, width)
    folded = max(plan.folded, 16)
    left = (parts, folded, width)
    return pl.pallas_call(
        functools.partial(kernel, plan),
        out_shape=jax.ShapeDtypeStruct((plan.own * lat, width), F32),
        in_specs=[hbm, hbm, hbm, smem, smem, vmem, vmem, vmem],
        out_specs=hbm,
        scratch_shapes=[
            pltpu.VMEM((lat + 1, pad, width), F32),
            pltpu.VMEM((parts * pad, lanes), BF16),
            pltpu.VMEM((2, parts * pad, lanes), BF16),
            pltpu.VMEM((parts * pad, lanes), BF16),
            pltpu.VMEM((parts * pad, lanes), BF16),
            pltpu.VMEM(tile, BF16), pltpu.VMEM((2,) + gathered, BF16), pltpu.VMEM(gathered, BF16), pltpu.VMEM(tile, BF16),
            pltpu.VMEM(left, BF16), pltpu.VMEM(left, BF16), pltpu.VMEM(left, BF16), pltpu.VMEM(left, BF16),
            pltpu.VMEM((parts * pad, parts * pad), BF16),
            pltpu.VMEM((round_up(parts * pad, 128), parts * plan.own), BF16),
            pltpu.VMEM((2 * tallest * lat, width), F32),
            pltpu.VMEM((2, tallest, lat, width), BF16),
            pltpu.VMEM((16 * lat, width), F32),
            pltpu.VMEM((5, pad, width), F32),
            pltpu.VMEM((lat, width), F32),
            pltpu.VMEM((lat, width), F32),
            pltpu.VMEM((lat, width), F32),
            pltpu.VMEM((lat, width), F32),
            pltpu.VMEM(filling, BF16),
            pltpu.VMEM((parts, tallest, spare), BF16),
            pltpu.VMEM((parts, tallest, spare), F32),
            pltpu.VMEM((folded, width), F32),
            pltpu.VMEM((parts * 16, lanes), F32),
            pltpu.VMEM((16, lanes), F32),
            pltpu.VMEM((positions, tallest, width), F32),
            pltpu.VMEM((positions, 2, tallest, width), F32),
            dma((2, CHUNKS, parts)),
            dma((2, CHUNKS, parts)),
            dma((2, CHUNKS, parts)),
            dma((2, CHUNKS, parts)),
            dma((2, parts)),
            dma((2, parts)),
            dma((positions, 2)),
            dma((positions, 2)),
            dma((2,)),
            dma((2,)),
            dma,
            dma((2, CHUNKS)),
            dma((2, CHUNKS)),
        ],
        compiler_params=pltpu.CompilerParams(
            collective_id=identity, has_side_effects=True, vmem_limit_bytes=62 * 1024 * 1024
        ),
    )(lam, source, mixing, drift_x, drift_y, ocean_mask, misfit, obs_mask)


def census_kernel(ring, plan, ocean_mask, most, mine, others, send_sem, recv_sem):
    lon = lax.axis_index("lon")
    rows = plan.rows
    barrier = pltpu.get_barrier_semaphore()
    for k in range(1, ring):
        pl.semaphore_signal(barrier, inc=1, device_id={"lon": lax.rem(lon + k, ring)}, device_id_type=MESH)
    worst = jnp.zeros((8, 128), F32)
    for b in range(plan.parts):
        count = jnp.sum(ocean_mask[b * rows : (b + 1) * rows].astype(F32))
        worst = worst + jnp.full((8, 128), jnp.maximum(count - plan.lanes, 0.0), F32)
    mine[...] = worst
    pl.semaphore_wait(barrier, ring - 1)

    def copy(k, arriving):
        other = lax.rem(lon + k, ring)
        place = other if arriving else lon
        return pltpu.make_async_remote_copy(
            src_ref=mine,
            dst_ref=others.at[place],
            send_sem=send_sem.at[k],
            recv_sem=recv_sem.at[place],
            device_id={"lon": other},
            device_id_type=MESH,
        )

    for k in range(1, ring):
        copy(k, False).start()
    for k in range(1, ring):
        copy(k, True).wait_recv()
        worst = jnp.maximum(worst, others[lax.rem(lon + k, ring)])
    for k in range(1, ring):
        copy(k, False).wait_send()
    most[...] = worst


def census(ring, plan, ocean_mask):
    vmem = pl.BlockSpec(memory_space=pltpu.VMEM)
    return pl.pallas_call(
        functools.partial(census_kernel, ring, plan),
        out_shape=jax.ShapeDtypeStruct((8, 128), F32),
        in_specs=[vmem],
        out_specs=vmem,
        scratch_shapes=[
            pltpu.VMEM((8, 128), F32),
            pltpu.VMEM((ring, 8, 128), F32),
            pltpu.SemaphoreType.DMA((ring,)),
            pltpu.SemaphoreType.DMA((ring,)),
        ],
        compiler_params=pltpu.CompilerParams(collective_id=0, has_side_effects=True),
    )(ocean_mask)


def per_device(
    parts, ring, lam_final, stored_source, mixing, drift_x, drift_y, ocean_mask, misfit, obs_mask
):
    steps = stored_source.shape[0]
    own, lat, width = lam_final.shape
    rows = lat // parts
    packed = Plan(steps, parts, ring, own, lat, width, rows * 3 // 4)
    whole = Plan(steps, parts, ring, own, lat, width, rows)
    most = census(ring, packed, ocean_mask)
    operands = (
        lam_final.reshape(own * lat, width), stored_source, mixing, drift_x, drift_y, ocean_mask, misfit, obs_mask
    )
    result = lax.cond(
        most[0, 0] <= width,
        functools.partial(call, packed, 1),
        functools.partial(call, whole, 2),
        *operands,
    )
    return result.reshape(own, lat, width)


def solution(mesh):
    in_specs = (
        P("spec", None, "lon"),
        P(None, "spec", None, "lon"),
        P(),
        P(),
        P(),
        P(None, "lon"),
        P(None, None, "lon"),
        P(None, None, "lon"),
    )
    out_specs = P("spec", None, "lon")
    return jax.shard_map(
        functools.partial(per_device, mesh.shape["spec"], mesh.shape["lon"]),
        mesh=mesh, in_specs=in_specs, out_specs=out_specs, check_vma=False,
    )
```

```python
import functools

import jax
import jax.numpy as jnp
from jax import lax
from jax.experimental import pallas as pl
from jax.experimental.pallas import tpu as pltpu
from jax.sharding import PartitionSpec as P

SHARES = (3, 5, 5, 5, 3)
CHUNKS = len(SHARES)
MESH = pl.DeviceIdType.MESH
F32, BF16 = jnp.float32, jnp.bfloat16


def round_up(value, unit):
    return -(-value // unit) * unit


class Plan:
    def __init__(self, steps, parts, ring, own, lat, width, base):
        self.steps, self.parts, self.ring = steps, parts, ring
        self.own, self.lat, self.width = own, lat, width
        self.rows = lat // parts
        self.base, self.over = base, self.rows - base
        self.lanes, self.spare = base * width, (self.rows - base) * width
        self.main = own // 16 * 16
        self.left = own - self.main
        self.keeper = parts // 2
        self.pad = round_up(own, 16)
        groups = self.pad // 16
        total = sum(SHARES)
        edges = [(groups * sum(SHARES[1:q]) + total // 2) // total * 16 for q in range(1, CHUNKS + 1)] + [self.main]
        self.bounds = [(edges[-2], edges[-1])] + list(zip(edges[:-2], edges[1:-1]))
        self.folded = round_up(base * self.left, 16)

    def span(self, q):
        low, high = self.bounds[q]
        held = high - low + (self.left if q == 0 else 0)
        return low, high - low, held, round_up(held, 16)

    @property
    def tallest(self):
        return max(self.span(q)[3] for q in range(CHUNKS))


def kernel(
    plan, lam, source, mixing, drift_x, drift_y, ocean_mask, misfit, obs_mask, out,
    state, sin, rin, sout, rout, sin_x, rin_x, sout_x, rout_x, sin_l, rin_l, sout_l, rout_l,
    weight_buf, mixing_buf, stage, source_buf, factor, coef, ocean, forcing, ids, shared_ids, fill, extra_in, extra_out, fold, mixed, lift,
    halo_send, halo_recv,
    send_sem, recv_sem, shared_send_sem, shared_recv_sem, left_send_sem, left_recv_sem, halo_send_sem, halo_recv_sem,
    stage_sem, source_sem, weight_sem, self_sem, shared_self_sem,
):
    me = lax.axis_index("spec")
    lon = lax.axis_index("lon")
    parts, ring, rows, lat, width = plan.parts, plan.ring, plan.rows, plan.lat, plan.width
    own, main, left, pad, lanes, base, over, spare = (
        plan.own, plan.main, plan.left, plan.pad, plan.lanes, plan.base, plan.over, plan.spare
    )
    steps, tallest = plan.steps, plan.tallest
    east, west = lax.rem(lon + 1, ring), lax.rem(lon + ring - 1, ring)
    peers = list(range(1, parts))
    order = [(step, q) for step in reversed(range(steps)) for q in range(CHUNKS)]
    lane = lax.broadcasted_iota(jnp.int32, (16, width), 1)

    def peer(offset):
        return lax.rem(me + offset, parts)

    def aligned(value):
        return pl.multiple_of(value, 16)

    def lam_copy(q):
        low, _, held, _ = plan.span(q)
        return pltpu.make_async_copy(
            lam.at[pl.ds(low * lat, held * lat)],
            stage.at[pl.ds((q % 2) * tallest * lat, held * lat)],
            stage_sem.at[q % 2],
        )

    def out_copy(q):
        low, _, held, _ = plan.span(q)
        return pltpu.make_async_copy(
            stage.at[pl.ds((q % 2) * tallest * lat, held * lat)],
            out.at[pl.ds(low * lat, held * lat)],
            stage_sem.at[q % 2],
        )

    def source_copy(position):
        step, q = order[position]
        low, _, held, _ = plan.span(q)
        return pltpu.make_async_copy(
            source.at[step, pl.ds(low, held)],
            source_buf.at[position % 2, pl.ds(0, held)],
            source_sem.at[position % 2],
        )

    mixing_copy = pltpu.make_async_copy(mixing, mixing_buf.at[pl.ds(0, parts * own)], weight_sem)

    def inward(slot, q, offset):
        low, count, _, _ = plan.span(q)
        target = peer(offset)
        return pltpu.make_async_remote_copy(
            src_ref=sin.at[pl.ds(aligned(target * pad + low), count)],
            dst_ref=rin.at[slot, pl.ds(aligned(me * pad + low), count)],
            send_sem=send_sem.at[0, q, offset],
            recv_sem=recv_sem.at[0, q, me],
            device_id={"spec": target},
            device_id_type=MESH,
        )

    def inward_arrival(slot, q, offset):
        low, count, _, _ = plan.span(q)
        origin = peer(offset)
        return pltpu.make_async_remote_copy(
            src_ref=sin.at[pl.ds(aligned(origin * pad + low), count)],
            dst_ref=rin.at[slot, pl.ds(aligned(origin * pad + low), count)],
            send_sem=send_sem.at[0, q, offset],
            recv_sem=recv_sem.at[0, q, origin],
            device_id={"spec": origin},
            device_id_type=MESH,
        )

    def inward_self(slot, q):
        low, count, _, _ = plan.span(q)
        return pltpu.make_async_copy(
            sin.at[pl.ds(aligned(me * pad + low), count)],
            rin.at[slot, pl.ds(aligned(me * pad + low), count)],
            self_sem.at[0, q],
        )

    def outward(q, offset):
        low, count, _, _ = plan.span(q)
        target = peer(offset)
        return pltpu.make_async_remote_copy(
            src_ref=sout.at[pl.ds(aligned(target * pad + low), count)],
            dst_ref=rout.at[pl.ds(aligned(me * pad + low), count)],
            send_sem=send_sem.at[1, q, offset],
            recv_sem=recv_sem.at[1, q, me],
            device_id={"spec": target},
            device_id_type=MESH,
        )

    def outward_arrival(q, offset):
        low, count, _, _ = plan.span(q)
        origin = peer(offset)
        return pltpu.make_async_remote_copy(
            src_ref=sout.at[pl.ds(aligned(origin * pad + low), count)],
            dst_ref=rout.at[pl.ds(aligned(origin * pad + low), count)],
            send_sem=send_sem.at[1, q, offset],
            recv_sem=recv_sem.at[1, q, origin],
            device_id={"spec": origin},
            device_id_type=MESH,
        )

    def outward_self(q):
        low, count, _, _ = plan.span(q)
        return pltpu.make_async_copy(
            sout.at[pl.ds(aligned(me * pad + low), count)],
            rout.at[pl.ds(aligned(me * pad + low), count)],
            self_sem.at[1, q],
        )

    keeper = plan.keeper

    def shared_in(slot, q, place):
        low, _, _, tall = plan.span(q)
        return pltpu.make_async_remote_copy(
            src_ref=sin_x.at[pl.ds(low, tall)],
            dst_ref=rin_x.at[slot, pl.ds(aligned(place * pad + low), tall)],
            send_sem=shared_send_sem.at[0, q, 0],
            recv_sem=shared_recv_sem.at[0, q, place],
            device_id={"spec": keeper},
            device_id_type=MESH,
        )

    def shared_in_self(slot, q):
        low, _, _, tall = plan.span(q)
        return pltpu.make_async_copy(
            sin_x.at[pl.ds(low, tall)],
            rin_x.at[slot, pl.ds(keeper * pad + low, tall)],
            shared_self_sem.at[0, q],
        )

    def shared_out(q, target, index):
        low, _, _, tall = plan.span(q)
        return pltpu.make_async_remote_copy(
            src_ref=sout_x.at[pl.ds(target * pad + low, tall)],
            dst_ref=rout_x.at[pl.ds(low, tall)],
            send_sem=shared_send_sem.at[1, q, index],
            recv_sem=shared_recv_sem.at[1, q, 0],
            device_id={"spec": target},
            device_id_type=MESH,
        )

    def shared_out_self(q):
        low, _, _, tall = plan.span(q)
        return pltpu.make_async_copy(
            sout_x.at[pl.ds(keeper * pad + low, tall)],
            rout_x.at[pl.ds(low, tall)],
            shared_self_sem.at[1, q],
        )

    others = [z for z in range(parts) if z != keeper]

    def leftover(phase, offset, arriving):
        sender, receiver = (sin_l, rin_l) if phase == 0 else (sout_l, rout_l)
        other = peer(offset)
        place = other if arriving else me
        return pltpu.make_async_remote_copy(
            src_ref=sender.at[other],
            dst_ref=receiver.at[place],
            send_sem=left_send_sem.at[phase, offset],
            recv_sem=left_recv_sem.at[phase, place],
            device_id={"spec": other},
            device_id_type=MESH,
        )

    def halo(position, group, side):
        place = pl.ds(aligned(group * 16), 16)
        return pltpu.make_async_remote_copy(
            src_ref=halo_send.at[position, place],
            dst_ref=halo_recv.at[position, side, place],
            send_sem=halo_send_sem.at[position, group, side],
            recv_sem=halo_recv_sem.at[position, group, side],
            device_id={"lon": west if side == 0 else east},
            device_id_type=MESH,
        )

    for q in range(min(2, CHUNKS)):
        lam_copy(q).start()
    mixing_copy.start()
    source_copy(0).start()
    source_copy(1).start()

    barrier = pltpu.get_barrier_semaphore()
    for offset in peers:
        pl.semaphore_signal(barrier, inc=1, device_id={"spec": peer(offset)}, device_id_type=MESH)
    for side in (west, east):
        pl.semaphore_signal(barrier, inc=1, device_id={"lon": side}, device_id_type=MESH)

    def set_forcing(step):
        forcing[...] = misfit[step] * obs_mask[step].astype(F32)

    wet = ocean_mask[...].astype(F32)
    ocean[...] = wet
    set_forcing(steps - 1)
    state[lat] = jnp.zeros((pad, width), F32)
    if left:
        lift[...] = jnp.zeros((16, lanes), F32)

    def column(numbering, row):
        return jnp.transpose(jnp.broadcast_to(numbering[pl.ds(row, 1)], (width, width)))

    def match(tall, row):
        return jnp.where(tall == ids[pl.ds(row, 1)], 1.0, 0.0).astype(BF16)

    if over:
        row_of = lax.broadcasted_iota(jnp.int32, (lat, width), 0)

        def block_of(index):
            return sum((index >= b * rows).astype(jnp.int32) for b in range(1, parts))

        riding = row_of - block_of(row_of) * rows >= base
        chosen = jnp.where(riding, wet, 1.0 - wet)
        here = lax.broadcasted_iota(jnp.int32, (lat, lat), 0)
        there = lax.broadcasted_iota(jnp.int32, (lat, lat), 1)
        block_here, block_there = block_of(here), block_of(there)
        kind_here = (here - block_here * rows >= base).astype(jnp.int32)
        kind_there = (there - block_there * rows >= base).astype(jnp.int32)
        before = (block_here == block_there) & (kind_here == kind_there) & (there < here)
        first = lax.broadcasted_iota(jnp.int32, (width, width), 0)
        second = lax.broadcasted_iota(jnp.int32, (width, width), 1)
        packed = chosen.astype(BF16)
        within = jnp.dot(packed, (first < second).astype(F32).astype(BF16), preferred_element_type=F32)
        totals = jnp.dot(packed, jnp.ones((width, width), BF16), preferred_element_type=F32)
        offset_rows = jnp.dot(
            before.astype(F32).astype(BF16), totals.astype(BF16), preferred_element_type=F32
        )
        rank = within + offset_rows
        ids[...] = jnp.where(chosen > 0.0, rank, jnp.where(riding, -1.0, -2.0))

        def count_of(kind):
            chosen_rows = ((block_here == block_there) & (kind_there == kind)).astype(F32).astype(BF16)
            return jnp.dot(chosen_rows, totals.astype(BF16), preferred_element_type=F32)

        dry = count_of(0)
        excess = jnp.maximum(count_of(1) - dry, 0.0)
        earlier = ((block_there < block_here) & (there == block_there * rows)).astype(F32).astype(BF16)
        ahead = jnp.dot(earlier, excess.astype(BF16), preferred_element_type=F32)
        shared_ids[...] = jnp.where(riding & (chosen > 0.0) & (rank >= dry), ahead + rank - dry, -1.0)
        numbers = lax.broadcasted_iota(jnp.int32, (width, width), 1).astype(F32)

        def fill_block(b, carry):
            for o in range(over):
                tall = column(ids, b * rows + base + o)
                spot = pl.ds(pl.multiple_of(b * spare + o * width, width), width)
                fill[spot, lanes:] = jnp.where(
                    column(shared_ids, b * rows + base + o) == numbers, 1.0, 0.0
                ).astype(BF16)

                def one(r, inner):
                    fill[spot, pl.ds(pl.multiple_of(r * width, width), width)] = match(tall, b * rows + r)
                    return inner

                lax.fori_loop(0, base, one, 0)
            return carry


    def emit(x, i, b, r, c, local):
        state[i, pl.ds(c, 16)] = x
        rounded = x.astype(BF16)
        if r < base:
            sin[pl.ds(aligned(b * pad + c), 16), r * width : (r + 1) * width] = rounded
        else:
            extra_in[b, pl.ds(local, 16), (r - base) * width : (r - base + 1) * width] = rounded

    def tiles(body):
        wide = lanes // (2 * width)

        def one(n, carry):
            body(pl.ds(pl.multiple_of(n * 2 * width, 2 * width), 2 * width))
            return carry

        lax.fori_loop(0, wide, one, 0)
        if wide * 2 * width < lanes:
            body(pl.ds(wide * 2 * width, width))

    def fold_rows(sender):
        def one(b, carry):
            value = sender[pl.ds(aligned(b * pad + main), 16), :].astype(F32)
            for t in range(base):
                fold[t * left : (t + 1) * left] = value[:left, t * width : (t + 1) * width]
            sin_l[b] = fold[...].astype(BF16)
            return carry

        lax.fori_loop(0, parts, one, 0)

    def send_inward(slot, q, first):
        low, count, held, tall = plan.span(q)
        ends = q == 0
        if over:

            def block(turn, carry):
                offset = parts - 1 - turn
                b = peer(offset)
                if first and q == 0:
                    fill_block(b, 0)
                place = pl.ds(aligned(b * pad + low), tall)

                def one(cols):
                    moved = jnp.dot(
                        extra_in[b, :tall],
                        fill[pl.ds(pl.multiple_of(b * spare, width), spare), cols],
                        preferred_element_type=F32,
                    )
                    sin[place, cols] = (sin[place, cols].astype(F32) + moved).astype(BF16)

                tiles(one)

                @pl.when(offset > 0)
                def _():
                    inward(slot, q, offset).start()

                return carry + jnp.dot(
                    extra_in[b, :tall],
                    fill[pl.ds(pl.multiple_of(b * spare, width), spare), lanes:],
                    preferred_element_type=F32,
                )

            tile = lax.fori_loop(0, parts, block, jnp.zeros((tall, width), F32))
            if held < tall:
                tile = jnp.where(lax.broadcasted_iota(jnp.int32, (tall, width), 0) < held, tile, 0.0)
            sin_x[low : low + tall] = tile.astype(BF16)

            @pl.when(me == keeper)
            def _():
                shared_in_self(slot, q).start()

            @pl.when(me != keeper)
            def _():
                shared_in(slot, q, me).start()

        else:
            for offset in peers:
                inward(slot, q, offset).start()
        inward_self(slot, q).start()
        if ends and left:
            if not first:
                for offset in peers:
                    leftover(0, offset, False).wait_send()
            fold_rows(sin)
            for offset in peers:
                leftover(0, offset, False).start()
            rin_l[me] = sin_l[me]

    for q in range(CHUNKS):
        low, count, held, tall = plan.span(q)
        lam_copy(q).wait()
        start = (q % 2) * tallest * lat

        def prepare(g, carry):
            def block(b, inner):
                for r in range(rows):
                    i = b * rows + r
                    a = stage[pl.ds(start + g * 16 * lat + i, 16, stride=lat)]
                    x = (a + forcing[pl.ds(i, 1)]) * ocean[pl.ds(i, 1)]
                    emit(x, i, b, r, aligned(low + g * 16), aligned(g * 16))
                return inner

            return lax.fori_loop(0, parts, block, carry)

        lax.fori_loop(0, tall // 16, prepare, 0)
        if q + 2 < CHUNKS:
            lam_copy(q + 2).start()
        if q == 0:
            pl.semaphore_wait(barrier, len(peers) + 2)
        send_inward((steps - 1) % 2, q, True)

    def coefficients(c, carry):
        speed_x = drift_x[me * own + c]
        speed_y = drift_y[me * own + c]
        values = (
            1.0 - jnp.abs(speed_x) - jnp.abs(speed_y),
            jnp.maximum(speed_x, 0.0), jnp.maximum(-speed_x, 0.0),
            jnp.maximum(speed_y, 0.0), jnp.maximum(-speed_y, 0.0),
        )
        for k, value in enumerate(values):
            coef[k, pl.ds(c, 1)] = jnp.full((1, width), value, F32)
        return carry

    lax.fori_loop(0, own, coefficients, 0)

    mixing_copy.wait()

    def arrange_weights():
        wide = mixing_buf.shape[0]
        start = 0
        pieces = [plan.bounds[q] for q in range(CHUNKS)] + ([(main, pad)] if left else [])
        for low, high in pieces:
            count = high - low
            picked = lax.broadcasted_iota(jnp.int32, (count, parts * own), 0) + low
            picking = lax.broadcasted_iota(jnp.int32, (count, parts * own), 1)
            place = lax.broadcasted_iota(jnp.int32, (count, wide), 1)

            def one(h, carry):
                pick = (picking == h * own + picked) & (picked < own)
                rows_of_home = lax.dot_general(
                    pick.astype(F32).astype(BF16), mixing_buf[...], (((1,), (1,)), ((), ())),
                    preferred_element_type=F32,
                )
                value = jnp.zeros((count, wide), F32)
                for o in range(parts):
                    shifted = pltpu.roll(rows_of_home, o * (pad - own), 1) if o and pad > own else rows_of_home
                    value = jnp.where((place >= o * pad) & (place < o * pad + own), shifted, value)
                weight_buf[pl.ds(aligned(start + h * count), count)] = value.astype(BF16)[:, : parts * pad]
                return carry

            lax.fori_loop(0, parts, one, 0)
            start += parts * count

    arrange_weights()

    for step in reversed(range(steps)):
        final = step == 0
        first = step == steps - 1
        slot = step % 2

        if left:
            for offset in peers:
                leftover(0, offset, True).wait_recv()

            def lift_rows(o, carry):
                value = rin_l[o].astype(F32)
                for t in range(base):
                    lift[:left, t * width : (t + 1) * width] = value[t * left : (t + 1) * left]
                rin[slot, pl.ds(aligned(o * pad + main), 16)] = lift[...].astype(BF16)
                return carry

            lax.fori_loop(0, parts, lift_rows, 0)

        for q in range(CHUNKS):
            inward_self(slot, q).wait()
            for offset in peers:
                inward_arrival(slot, q, offset).wait_recv()
        if over:

            @pl.when(me == keeper)
            def _():
                for q in range(CHUNKS):
                    shared_in_self(slot, q).wait()
                    for z in others:
                        shared_in(slot, q, z).wait_recv()

        start = 0
        for q in range(CHUNKS):
            low, count, held, tall = plan.span(q)
            ends = q == 0
            if not first:
                for offset in peers:
                    outward(q, offset).wait_send()

            def couple(cols):
                result = jnp.dot(
                    weight_buf[start : start + parts * count], rin[slot, :, cols], preferred_element_type=F32
                )
                for h in range(parts):
                    sout[h * pad + low : h * pad + low + count, cols] = result[h * count : (h + 1) * count].astype(BF16)

            tiles(couple)
            outward_self(q).start()
            for offset in peers:
                outward(q, offset).start()
            start += parts * count
            if ends and left:
                if not first:
                    for offset in peers:
                        leftover(1, offset, False).wait_send()

                def couple_left(cols):
                    mixed[:, cols] = jnp.dot(
                        weight_buf[parts * main :], rin[slot, :, cols], preferred_element_type=F32
                    )

                tiles(couple_left)
                for h in range(parts):
                    for t in range(base):
                        fold[t * left : (t + 1) * left] = mixed[
                            h * 16 : h * 16 + left, t * width : (t + 1) * width
                        ]
                    sout_l[h] = fold[...].astype(BF16)
                for offset in peers:
                    leftover(1, offset, False).start()
                rout_l[me] = sout_l[me]
            if over:

                @pl.when(me == keeper)
                def _():
                    if not first:
                        for index, target in enumerate(others):
                            shared_out(q, target, index).wait_send()
                    begin = start - parts * count
                    result = jnp.dot(
                        weight_buf[begin : begin + parts * count], rin_x[slot], preferred_element_type=F32
                    ).astype(BF16)
                    for h in range(parts):
                        sout_x[h * pad + low : h * pad + low + count] = result[h * count : (h + 1) * count]
                    if ends and left:
                        tail = jnp.dot(
                            weight_buf[parts * main :], rin_x[slot], preferred_element_type=F32
                        ).astype(BF16)
                        for h in range(parts):
                            sout_x[h * pad + main : h * pad + pad] = tail[h * 16 : (h + 1) * 16]
                    shared_out_self(q).start()
                    for index, target in enumerate(others):
                        shared_out(q, target, index).start()

        if not final:
            set_forcing(step - 1)
        for q in range(CHUNKS):
            low, count, held, tall = plan.span(q)
            ends = q == 0
            position = (steps - 1 - step) * CHUNKS + q
            source_slot = position % 2
            source_copy(position).wait()
            outward_self(q).wait()
            for offset in peers:
                outward_arrival(q, offset).wait_recv()
            if ends and left:
                for offset in peers:
                    leftover(1, offset, True).wait_recv()

                def spread(b, carry):
                    value = rout_l[b].astype(F32)
                    for t in range(base):
                        lift[:left, t * width : (t + 1) * width] = value[t * left : (t + 1) * left]
                    rout[pl.ds(aligned(b * pad + main), 16)] = lift[...].astype(BF16)
                    return carry

                lax.fori_loop(0, parts, spread, 0)
            if over:

                @pl.when(me == keeper)
                def _():
                    shared_out_self(q).wait()

                @pl.when(me != keeper)
                def _():
                    shared_out(q, keeper, 0).wait_recv()

                def restore(b, carry):
                    spot = pl.ds(pl.multiple_of(b * spare, width), spare)
                    across = (((1,), (1,)), ((), ()))
                    extra_out[b, :tall] = lax.dot_general(
                        rout[pl.ds(aligned(b * pad + low), tall)], fill[spot, :lanes], across,
                        preferred_element_type=F32,
                    ) + lax.dot_general(
                        rout_x[low : low + tall], fill[spot, lanes:], across, preferred_element_type=F32
                    )
                    return carry

                lax.fori_loop(0, parts, restore, 0)

            def update(g, carry):
                c = aligned(low + g * 16)
                local = aligned(g * 16)
                for k in range(16):
                    factor[k * lat : (k + 1) * lat] = source_buf[source_slot, local + k].astype(F32)

                def block(b, edges):
                    tips = edges
                    for r in range(rows):
                        i = b * rows + r
                        if r < base:
                            coupled = rout[
                                pl.ds(aligned(b * pad + c), 16), r * width : (r + 1) * width
                            ].astype(F32)
                            if over:
                                coupled = coupled * ocean[pl.ds(i, 1)]
                        else:
                            coupled = extra_out[b, pl.ds(local, 16), (r - base) * width : (r - base + 1) * width]
                        adjoint = state[i, pl.ds(c, 16)] + factor[pl.ds(i, 16, stride=lat)] * coupled
                        state[i, pl.ds(c, 16)] = adjoint
                        place = lane - 2 * i
                        tips = jnp.where((place == 0) | (place == 1), pltpu.roll(adjoint, 2 * i + 1, 1), tips)
                    return tips

                halo_send[position, pl.ds(local, 16)] = lax.fori_loop(
                    0, parts, block, jnp.zeros((16, width), F32)
                )
                halo(position, g, 0).start()
                halo(position, g, 1).start()
                return carry

            lax.fori_loop(0, tall // 16, update, 0)
            if position + 2 < len(order):
                source_copy(position + 2).start()
            if final:
                if q >= 2:
                    out_copy(q - 2).wait()
            else:
                for offset in peers:
                    inward(slot, q, offset).wait_send()
                if over:

                    @pl.when(me != keeper)
                    def _():
                        shared_in(slot, q, me).wait_send()

            begin = (q % 2) * tallest * lat

            def advect(g, carry):
                c = aligned(low + g * 16)
                local = aligned(g * 16)
                halo(position, g, 0).wait()
                halo(position, g, 1).wait()
                stay, px, nx, py, ny = (coef[k, pl.ds(c, 16)] for k in range(5))
                both = jnp.where(
                    lane % 2 == 1,
                    pltpu.roll(halo_recv[position, 0, pl.ds(local, 16)], width - 2, 1),
                    halo_recv[position, 1, pl.ds(local, 16)],
                )

                def block(b, state_of):
                    southern, adjoint = state_of
                    tips = pltpu.roll(both, (width - 2 * b * rows) % width, 1)
                    for r in range(rows):
                        i = b * rows + r
                        northern = state[i + 1, pl.ds(c, 16)]
                        tip = pltpu.roll(tips, width - 2 * r, 1) if r else tips
                        eastern = jnp.where(lane == width - 1, tip, pltpu.roll(adjoint, width - 1, 1))
                        western = jnp.where(lane == 0, tip, pltpu.roll(adjoint, 1, 1))
                        result = stay * adjoint + px * eastern + nx * western
                        result = result + py * northern + ny * southern
                        if final:
                            stage[pl.ds(begin + local * lat + i, 16, stride=lat)] = result
                        else:
                            emit((result + forcing[pl.ds(i, 1)]) * ocean[pl.ds(i, 1)], i, b, r, c, local)
                        southern, adjoint = adjoint, northern
                    return southern, adjoint

                lax.fori_loop(0, parts, block, (jnp.zeros((16, width), F32), state[0, pl.ds(c, 16)]))
                return carry

            lax.fori_loop(0, tall // 16, advect, 0)
            if final:
                out_copy(q).start()
            else:
                send_inward((step - 1) % 2, q, False)

    for q in range(CHUNKS):
        for offset in peers:
            inward(0, q, offset).wait_send()
            outward(q, offset).wait_send()
        if over:

            @pl.when(me == keeper)
            def _():
                for index, target in enumerate(others):
                    shared_out(q, target, index).wait_send()

            @pl.when(me != keeper)
            def _():
                shared_in(0, q, me).wait_send()

    if left:
        for offset in peers:
            leftover(0, offset, False).wait_send()
            leftover(1, offset, False).wait_send()
    for q in range(max(CHUNKS - 2, 0), CHUNKS):
        out_copy(q).wait()


def call(plan, identity, lam, source, mixing, drift_x, drift_y, ocean_mask, misfit, obs_mask):
    vmem = pl.BlockSpec(memory_space=pltpu.VMEM)
    smem = pl.BlockSpec(memory_space=pltpu.SMEM)
    hbm = pl.BlockSpec(memory_space=pl.ANY)
    dma = pltpu.SemaphoreType.DMA
    parts, pad, lanes, lat, width = plan.parts, plan.pad, plan.lanes, plan.lat, plan.width
    tallest = plan.tallest
    positions = plan.steps * CHUNKS
    spare = max(plan.spare, width)
    filling = (parts * spare, lanes + width) if plan.over else (16, width)
    tile = (pad, width) if plan.over else (16, width)
    gathered = (parts * pad, width) if plan.over else (16, width)
    folded = max(plan.folded, 16)
    left = (parts, folded, width)
    return pl.pallas_call(
        functools.partial(kernel, plan),
        out_shape=jax.ShapeDtypeStruct((plan.own * lat, width), F32),
        in_specs=[hbm, hbm, hbm, smem, smem, vmem, vmem, vmem],
        out_specs=hbm,
        scratch_shapes=[
            pltpu.VMEM((lat + 1, pad, width), F32),
            pltpu.VMEM((parts * pad, lanes), BF16),
            pltpu.VMEM((2, parts * pad, lanes), BF16),
            pltpu.VMEM((parts * pad, lanes), BF16),
            pltpu.VMEM((parts * pad, lanes), BF16),
            pltpu.VMEM(tile, BF16), pltpu.VMEM((2,) + gathered, BF16), pltpu.VMEM(gathered, BF16), pltpu.VMEM(tile, BF16),
            pltpu.VMEM(left, BF16), pltpu.VMEM(left, BF16), pltpu.VMEM(left, BF16), pltpu.VMEM(left, BF16),
            pltpu.VMEM((parts * pad, parts * pad), BF16),
            pltpu.VMEM((round_up(parts * pad, 128), parts * plan.own), BF16),
            pltpu.VMEM((2 * tallest * lat, width), F32),
            pltpu.VMEM((2, tallest, lat, width), BF16),
            pltpu.VMEM((16 * lat, width), F32),
            pltpu.VMEM((5, pad, width), F32),
            pltpu.VMEM((lat, width), F32),
            pltpu.VMEM((lat, width), F32),
            pltpu.VMEM((lat, width), F32),
            pltpu.VMEM((lat, width), F32),
            pltpu.VMEM(filling, BF16),
            pltpu.VMEM((parts, tallest, spare), BF16),
            pltpu.VMEM((parts, tallest, spare), F32),
            pltpu.VMEM((folded, width), F32),
            pltpu.VMEM((parts * 16, lanes), F32),
            pltpu.VMEM((16, lanes), F32),
            pltpu.VMEM((positions, tallest, width), F32),
            pltpu.VMEM((positions, 2, tallest, width), F32),
            dma((2, CHUNKS, parts)),
            dma((2, CHUNKS, parts)),
            dma((2, CHUNKS, parts)),
            dma((2, CHUNKS, parts)),
            dma((2, parts)),
            dma((2, parts)),
            dma((positions, tallest // 16, 2)),
            dma((positions, tallest // 16, 2)),
            dma((2,)),
            dma((2,)),
            dma,
            dma((2, CHUNKS)),
            dma((2, CHUNKS)),
        ],
        compiler_params=pltpu.CompilerParams(
            collective_id=identity, has_side_effects=True, vmem_limit_bytes=62 * 1024 * 1024
        ),
    )(lam, source, mixing, drift_x, drift_y, ocean_mask, misfit, obs_mask)


def census_kernel(ring, plan, ocean_mask, most, mine, others, send_sem, recv_sem):
    lon = lax.axis_index("lon")
    rows = plan.rows
    barrier = pltpu.get_barrier_semaphore()
    for k in range(1, ring):
        pl.semaphore_signal(barrier, inc=1, device_id={"lon": lax.rem(lon + k, ring)}, device_id_type=MESH)
    worst = jnp.zeros((8, 128), F32)
    for b in range(plan.parts):
        count = jnp.sum(ocean_mask[b * rows : (b + 1) * rows].astype(F32))
        worst = worst + jnp.full((8, 128), jnp.maximum(count - plan.lanes, 0.0), F32)
    mine[...] = worst
    pl.semaphore_wait(barrier, ring - 1)

    def copy(k, arriving):
        other = lax.rem(lon + k, ring)
        place = other if arriving else lon
        return pltpu.make_async_remote_copy(
            src_ref=mine,
            dst_ref=others.at[place],
            send_sem=send_sem.at[k],
            recv_sem=recv_sem.at[place],
            device_id={"lon": other},
            device_id_type=MESH,
        )

    for k in range(1, ring):
        copy(k, False).start()
    for k in range(1, ring):
        copy(k, True).wait_recv()
        worst = jnp.maximum(worst, others[lax.rem(lon + k, ring)])
    for k in range(1, ring):
        copy(k, False).wait_send()
    most[0] = jnp.max(worst)


def census(ring, plan, ocean_mask):
    vmem = pl.BlockSpec(memory_space=pltpu.VMEM)
    return pl.pallas_call(
        functools.partial(census_kernel, ring, plan),
        out_shape=jax.ShapeDtypeStruct((1,), F32),
        in_specs=[vmem],
        out_specs=pl.BlockSpec(memory_space=pltpu.SMEM),
        scratch_shapes=[
            pltpu.VMEM((8, 128), F32),
            pltpu.VMEM((ring, 8, 128), F32),
            pltpu.SemaphoreType.DMA((ring,)),
            pltpu.SemaphoreType.DMA((ring,)),
        ],
        compiler_params=pltpu.CompilerParams(collective_id=0, has_side_effects=True),
    )(ocean_mask)


def per_device(
    parts, ring, lam_final, stored_source, mixing, drift_x, drift_y, ocean_mask, misfit, obs_mask
):
    steps = stored_source.shape[0]
    own, lat, width = lam_final.shape
    rows = lat // parts
    packed = Plan(steps, parts, ring, own, lat, width, rows * 3 // 4)
    whole = Plan(steps, parts, ring, own, lat, width, rows)
    most = census(ring, packed, ocean_mask)
    operands = (
        lam_final.reshape(own * lat, width), stored_source, mixing, drift_x, drift_y, ocean_mask, misfit, obs_mask
    )
    result = lax.cond(
        most[0] <= width,
        functools.partial(call, packed, 1),
        functools.partial(call, whole, 2),
        *operands,
    )
    return result.reshape(own, lat, width)


def solution(mesh):
    in_specs = (
        P("spec", None, "lon"),
        P(None, "spec", None, "lon"),
        P(),
        P(),
        P(),
        P(None, "lon"),
        P(None, None, "lon"),
        P(None, None, "lon"),
    )
    out_specs = P("spec", None, "lon")
    return jax.shard_map(
        functools.partial(per_device, mesh.shape["spec"], mesh.shape["lon"]),
        mesh=mesh, in_specs=in_specs, out_specs=out_specs, check_vma=False,
    )
```

```python
import functools

import jax
import jax.numpy as jnp
from jax import lax
from jax.experimental import pallas as pl
from jax.experimental.pallas import tpu as pltpu
from jax.sharding import PartitionSpec as P

SHARES = (3, 4, 4, 4, 4, 2)
CHUNKS = len(SHARES)
MESH = pl.DeviceIdType.MESH
F32, BF16 = jnp.float32, jnp.bfloat16


def round_up(value, unit):
    return -(-value // unit) * unit


class Plan:
    def __init__(self, steps, parts, ring, own, lat, width, base):
        self.steps, self.parts, self.ring = steps, parts, ring
        self.own, self.lat, self.width = own, lat, width
        self.rows = lat // parts
        self.base, self.over = base, self.rows - base
        self.lanes, self.spare = base * width, (self.rows - base) * width
        self.main = own // 16 * 16
        self.left = own - self.main
        self.keeper = parts // 2
        self.pad = round_up(own, 16)
        groups = self.pad // 16
        total = sum(SHARES)
        edges = [(groups * sum(SHARES[1:q]) + total // 2) // total * 16 for q in range(1, CHUNKS + 1)] + [self.main]
        self.bounds = [(edges[-2], edges[-1])] + list(zip(edges[:-2], edges[1:-1]))
        self.folded = round_up(base * self.left, 16)

    def span(self, q):
        low, high = self.bounds[q]
        held = high - low + (self.left if q == 0 else 0)
        return low, high - low, held, round_up(held, 16)

    @property
    def tallest(self):
        return max(self.span(q)[3] for q in range(CHUNKS))


def kernel(
    plan, lam, source, mixing, drift_x, drift_y, ocean_mask, misfit, obs_mask, out,
    state, sin, rin, sout, rout, sin_x, rin_x, sout_x, rout_x, sin_l, rin_l, sout_l, rout_l,
    weight_buf, mixing_buf, stage, source_buf, factor, coef, ocean, forcing, ids, shared_ids, fill, extra_in, extra_out, fold, mixed, lift,
    halo_send, halo_recv,
    send_sem, recv_sem, shared_send_sem, shared_recv_sem, left_send_sem, left_recv_sem, halo_send_sem, halo_recv_sem,
    stage_sem, source_sem, weight_sem, self_sem, shared_self_sem,
):
    me = lax.axis_index("spec")
    lon = lax.axis_index("lon")
    parts, ring, rows, lat, width = plan.parts, plan.ring, plan.rows, plan.lat, plan.width
    own, main, left, pad, lanes, base, over, spare = (
        plan.own, plan.main, plan.left, plan.pad, plan.lanes, plan.base, plan.over, plan.spare
    )
    steps, tallest = plan.steps, plan.tallest
    east, west = lax.rem(lon + 1, ring), lax.rem(lon + ring - 1, ring)
    peers = list(range(1, parts))
    order = [(step, q) for step in reversed(range(steps)) for q in range(CHUNKS)]
    lane = lax.broadcasted_iota(jnp.int32, (16, width), 1)

    def peer(offset):
        return lax.rem(me + offset, parts)

    def aligned(value):
        return pl.multiple_of(value, 16)

    def lam_copy(q):
        low, _, held, _ = plan.span(q)
        return pltpu.make_async_copy(
            lam.at[pl.ds(low * lat, held * lat)],
            stage.at[pl.ds((q % 2) * tallest * lat, held * lat)],
            stage_sem.at[q % 2],
        )

    def out_copy(q):
        low, _, held, _ = plan.span(q)
        return pltpu.make_async_copy(
            stage.at[pl.ds((q % 2) * tallest * lat, held * lat)],
            out.at[pl.ds(low * lat, held * lat)],
            stage_sem.at[q % 2],
        )

    def source_copy(position):
        step, q = order[position]
        low, _, held, _ = plan.span(q)
        return pltpu.make_async_copy(
            source.at[step, pl.ds(low, held)],
            source_buf.at[position % 2, pl.ds(0, held)],
            source_sem.at[position % 2],
        )

    mixing_copy = pltpu.make_async_copy(mixing, mixing_buf.at[pl.ds(0, parts * own)], weight_sem)

    def inward(slot, q, offset):
        low, count, _, _ = plan.span(q)
        target = peer(offset)
        return pltpu.make_async_remote_copy(
            src_ref=sin.at[pl.ds(aligned(target * pad + low), count)],
            dst_ref=rin.at[slot, pl.ds(aligned(me * pad + low), count)],
            send_sem=send_sem.at[0, q, offset],
            recv_sem=recv_sem.at[0, q, me],
            device_id={"spec": target},
            device_id_type=MESH,
        )

    def inward_arrival(slot, q, offset):
        low, count, _, _ = plan.span(q)
        origin = peer(offset)
        return pltpu.make_async_remote_copy(
            src_ref=sin.at[pl.ds(aligned(origin * pad + low), count)],
            dst_ref=rin.at[slot, pl.ds(aligned(origin * pad + low), count)],
            send_sem=send_sem.at[0, q, offset],
            recv_sem=recv_sem.at[0, q, origin],
            device_id={"spec": origin},
            device_id_type=MESH,
        )

    def inward_self(slot, q):
        low, count, _, _ = plan.span(q)
        return pltpu.make_async_copy(
            sin.at[pl.ds(aligned(me * pad + low), count)],
            rin.at[slot, pl.ds(aligned(me * pad + low), count)],
            self_sem.at[0, q],
        )

    def outward(q, offset):
        low, count, _, _ = plan.span(q)
        target = peer(offset)
        return pltpu.make_async_remote_copy(
            src_ref=sout.at[pl.ds(aligned(target * pad + low), count)],
            dst_ref=rout.at[pl.ds(aligned(me * pad + low), count)],
            send_sem=send_sem.at[1, q, offset],
            recv_sem=recv_sem.at[1, q, me],
            device_id={"spec": target},
            device_id_type=MESH,
        )

    def outward_arrival(q, offset):
        low, count, _, _ = plan.span(q)
        origin = peer(offset)
        return pltpu.make_async_remote_copy(
            src_ref=sout.at[pl.ds(aligned(origin * pad + low), count)],
            dst_ref=rout.at[pl.ds(aligned(origin * pad + low), count)],
            send_sem=send_sem.at[1, q, offset],
            recv_sem=recv_sem.at[1, q, origin],
            device_id={"spec": origin},
            device_id_type=MESH,
        )

    def outward_self(q):
        low, count, _, _ = plan.span(q)
        return pltpu.make_async_copy(
            sout.at[pl.ds(aligned(me * pad + low), count)],
            rout.at[pl.ds(aligned(me * pad + low), count)],
            self_sem.at[1, q],
        )

    keeper = plan.keeper

    def shared_in(slot, q, place):
        low, _, _, tall = plan.span(q)
        return pltpu.make_async_remote_copy(
            src_ref=sin_x.at[pl.ds(low, tall)],
            dst_ref=rin_x.at[slot, pl.ds(aligned(place * pad + low), tall)],
            send_sem=shared_send_sem.at[0, q, 0],
            recv_sem=shared_recv_sem.at[0, q, place],
            device_id={"spec": keeper},
            device_id_type=MESH,
        )

    def shared_in_self(slot, q):
        low, _, _, tall = plan.span(q)
        return pltpu.make_async_copy(
            sin_x.at[pl.ds(low, tall)],
            rin_x.at[slot, pl.ds(keeper * pad + low, tall)],
            shared_self_sem.at[0, q],
        )

    def shared_out(q, target, index):
        low, _, _, tall = plan.span(q)
        return pltpu.make_async_remote_copy(
            src_ref=sout_x.at[pl.ds(target * pad + low, tall)],
            dst_ref=rout_x.at[pl.ds(low, tall)],
            send_sem=shared_send_sem.at[1, q, index],
            recv_sem=shared_recv_sem.at[1, q, 0],
            device_id={"spec": target},
            device_id_type=MESH,
        )

    def shared_out_self(q):
        low, _, _, tall = plan.span(q)
        return pltpu.make_async_copy(
            sout_x.at[pl.ds(keeper * pad + low, tall)],
            rout_x.at[pl.ds(low, tall)],
            shared_self_sem.at[1, q],
        )

    others = [z for z in range(parts) if z != keeper]

    def leftover(phase, offset, arriving):
        sender, receiver = (sin_l, rin_l) if phase == 0 else (sout_l, rout_l)
        other = peer(offset)
        place = other if arriving else me
        return pltpu.make_async_remote_copy(
            src_ref=sender.at[other],
            dst_ref=receiver.at[place],
            send_sem=left_send_sem.at[phase, offset],
            recv_sem=left_recv_sem.at[phase, place],
            device_id={"spec": other},
            device_id_type=MESH,
        )

    def halo(position, group, side):
        place = pl.ds(aligned(group * 16), 16)
        return pltpu.make_async_remote_copy(
            src_ref=halo_send.at[position, place],
            dst_ref=halo_recv.at[position, side, place],
            send_sem=halo_send_sem.at[position, group, side],
            recv_sem=halo_recv_sem.at[position, group, side],
            device_id={"lon": west if side == 0 else east},
            device_id_type=MESH,
        )

    for q in range(min(2, CHUNKS)):
        lam_copy(q).start()
    mixing_copy.start()
    source_copy(0).start()
    source_copy(1).start()

    barrier = pltpu.get_barrier_semaphore()
    for offset in peers:
        pl.semaphore_signal(barrier, inc=1, device_id={"spec": peer(offset)}, device_id_type=MESH)
    for side in (west, east):
        pl.semaphore_signal(barrier, inc=1, device_id={"lon": side}, device_id_type=MESH)

    def set_forcing(step):
        forcing[...] = misfit[step] * obs_mask[step].astype(F32)

    wet = ocean_mask[...].astype(F32)
    ocean[...] = wet
    set_forcing(steps - 1)
    state[lat] = jnp.zeros((pad, width), F32)
    if left:
        lift[...] = jnp.zeros((16, lanes), F32)

    def column(numbering, row):
        return jnp.transpose(jnp.broadcast_to(numbering[pl.ds(row, 1)], (width, width)))

    def match(tall, row):
        return jnp.where(tall == ids[pl.ds(row, 1)], 1.0, 0.0).astype(BF16)

    if over:
        row_of = lax.broadcasted_iota(jnp.int32, (lat, width), 0)

        def block_of(index):
            return sum((index >= b * rows).astype(jnp.int32) for b in range(1, parts))

        riding = row_of - block_of(row_of) * rows >= base
        chosen = jnp.where(riding, wet, 1.0 - wet)
        here = lax.broadcasted_iota(jnp.int32, (lat, lat), 0)
        there = lax.broadcasted_iota(jnp.int32, (lat, lat), 1)
        block_here, block_there = block_of(here), block_of(there)
        kind_here = (here - block_here * rows >= base).astype(jnp.int32)
        kind_there = (there - block_there * rows >= base).astype(jnp.int32)
        before = (block_here == block_there) & (kind_here == kind_there) & (there < here)
        first = lax.broadcasted_iota(jnp.int32, (width, width), 0)
        second = lax.broadcasted_iota(jnp.int32, (width, width), 1)
        packed = chosen.astype(BF16)
        within = jnp.dot(packed, (first < second).astype(F32).astype(BF16), preferred_element_type=F32)
        totals = jnp.dot(packed, jnp.ones((width, width), BF16), preferred_element_type=F32)
        offset_rows = jnp.dot(
            before.astype(F32).astype(BF16), totals.astype(BF16), preferred_element_type=F32
        )
        rank = within + offset_rows
        ids[...] = jnp.where(chosen > 0.0, rank, jnp.where(riding, -1.0, -2.0))

        def count_of(kind):
            chosen_rows = ((block_here == block_there) & (kind_there == kind)).astype(F32).astype(BF16)
            return jnp.dot(chosen_rows, totals.astype(BF16), preferred_element_type=F32)

        dry = count_of(0)
        excess = jnp.maximum(count_of(1) - dry, 0.0)
        earlier = ((block_there < block_here) & (there == block_there * rows)).astype(F32).astype(BF16)
        ahead = jnp.dot(earlier, excess.astype(BF16), preferred_element_type=F32)
        shared_ids[...] = jnp.where(riding & (chosen > 0.0) & (rank >= dry), ahead + rank - dry, -1.0)
        numbers = lax.broadcasted_iota(jnp.int32, (width, width), 1).astype(F32)

        def fill_block(b, carry):
            for o in range(over):
                tall = column(ids, b * rows + base + o)
                spot = pl.ds(pl.multiple_of(b * spare + o * width, width), width)
                fill[spot, lanes:] = jnp.where(
                    column(shared_ids, b * rows + base + o) == numbers, 1.0, 0.0
                ).astype(BF16)

                def one(r, inner):
                    fill[spot, pl.ds(pl.multiple_of(r * width, width), width)] = match(tall, b * rows + r)
                    return inner

                lax.fori_loop(0, base, one, 0)
            return carry


    def emit(x, i, b, r, c, local):
        state[i, pl.ds(c, 16)] = x
        rounded = x.astype(BF16)
        if r < base:
            sin[pl.ds(aligned(b * pad + c), 16), r * width : (r + 1) * width] = rounded
        else:
            extra_in[b, pl.ds(local, 16), (r - base) * width : (r - base + 1) * width] = rounded

    def tiles(body):
        wide = lanes // (2 * width)

        def one(n, carry):
            body(pl.ds(pl.multiple_of(n * 2 * width, 2 * width), 2 * width))
            return carry

        lax.fori_loop(0, wide, one, 0)
        if wide * 2 * width < lanes:
            body(pl.ds(wide * 2 * width, width))

    def fold_rows(sender):
        def one(b, carry):
            value = sender[pl.ds(aligned(b * pad + main), 16), :].astype(F32)
            for t in range(base):
                fold[t * left : (t + 1) * left] = value[:left, t * width : (t + 1) * width]
            sin_l[b] = fold[...].astype(BF16)
            return carry

        lax.fori_loop(0, parts, one, 0)

    def send_inward(slot, q, first):
        low, count, held, tall = plan.span(q)
        ends = q == 0
        if over:

            def block(turn, carry):
                offset = parts - 1 - turn
                b = peer(offset)
                if first and q == 0:
                    fill_block(b, 0)
                place = pl.ds(aligned(b * pad + low), tall)

                def one(cols):
                    moved = jnp.dot(
                        extra_in[b, :tall],
                        fill[pl.ds(pl.multiple_of(b * spare, width), spare), cols],
                        preferred_element_type=F32,
                    )
                    sin[place, cols] = (sin[place, cols].astype(F32) + moved).astype(BF16)

                tiles(one)

                @pl.when(offset > 0)
                def _():
                    inward(slot, q, offset).start()

                return carry + jnp.dot(
                    extra_in[b, :tall],
                    fill[pl.ds(pl.multiple_of(b * spare, width), spare), lanes:],
                    preferred_element_type=F32,
                )

            tile = lax.fori_loop(0, parts, block, jnp.zeros((tall, width), F32))
            if held < tall:
                tile = jnp.where(lax.broadcasted_iota(jnp.int32, (tall, width), 0) < held, tile, 0.0)
            sin_x[low : low + tall] = tile.astype(BF16)

            @pl.when(me == keeper)
            def _():
                shared_in_self(slot, q).start()

            @pl.when(me != keeper)
            def _():
                shared_in(slot, q, me).start()

        else:
            for offset in peers:
                inward(slot, q, offset).start()
        inward_self(slot, q).start()
        if ends and left:
            if not first:
                for offset in peers:
                    leftover(0, offset, False).wait_send()
            fold_rows(sin)
            for offset in peers:
                leftover(0, offset, False).start()
            rin_l[me] = sin_l[me]

    for q in range(CHUNKS):
        low, count, held, tall = plan.span(q)
        lam_copy(q).wait()
        start = (q % 2) * tallest * lat

        def prepare(g, carry):
            def block(b, inner):
                for r in range(rows):
                    i = b * rows + r
                    a = stage[pl.ds(start + g * 16 * lat + i, 16, stride=lat)]
                    x = (a + forcing[pl.ds(i, 1)]) * ocean[pl.ds(i, 1)]
                    emit(x, i, b, r, aligned(low + g * 16), aligned(g * 16))
                return inner

            return lax.fori_loop(0, parts, block, carry)

        lax.fori_loop(0, tall // 16, prepare, 0)
        if q + 2 < CHUNKS:
            lam_copy(q + 2).start()
        if q == 0:
            pl.semaphore_wait(barrier, len(peers) + 2)
        send_inward((steps - 1) % 2, q, True)

    def coefficients(c, carry):
        speed_x = drift_x[me * own + c]
        speed_y = drift_y[me * own + c]
        values = (
            1.0 - jnp.abs(speed_x) - jnp.abs(speed_y),
            jnp.maximum(speed_x, 0.0), jnp.maximum(-speed_x, 0.0),
            jnp.maximum(speed_y, 0.0), jnp.maximum(-speed_y, 0.0),
        )
        for k, value in enumerate(values):
            coef[k, pl.ds(c, 1)] = jnp.full((1, width), value, F32)
        return carry

    lax.fori_loop(0, own, coefficients, 0)

    mixing_copy.wait()

    def arrange_weights():
        wide = mixing_buf.shape[0]
        start = 0
        pieces = [plan.bounds[q] for q in range(CHUNKS)] + ([(main, pad)] if left else [])
        for low, high in pieces:
            count = high - low
            picked = lax.broadcasted_iota(jnp.int32, (count, parts * own), 0) + low
            picking = lax.broadcasted_iota(jnp.int32, (count, parts * own), 1)
            place = lax.broadcasted_iota(jnp.int32, (count, wide), 1)

            def one(h, carry):
                pick = (picking == h * own + picked) & (picked < own)
                rows_of_home = lax.dot_general(
                    pick.astype(F32).astype(BF16), mixing_buf[...], (((1,), (1,)), ((), ())),
                    preferred_element_type=F32,
                )
                value = jnp.zeros((count, wide), F32)
                for o in range(parts):
                    shifted = pltpu.roll(rows_of_home, o * (pad - own), 1) if o and pad > own else rows_of_home
                    value = jnp.where((place >= o * pad) & (place < o * pad + own), shifted, value)
                weight_buf[pl.ds(aligned(start + h * count), count)] = value.astype(BF16)[:, : parts * pad]
                return carry

            lax.fori_loop(0, parts, one, 0)
            start += parts * count

    arrange_weights()

    for step in reversed(range(steps)):
        final = step == 0
        first = step == steps - 1
        slot = step % 2

        if left:
            for offset in peers:
                leftover(0, offset, True).wait_recv()

            def lift_rows(o, carry):
                value = rin_l[o].astype(F32)
                for t in range(base):
                    lift[:left, t * width : (t + 1) * width] = value[t * left : (t + 1) * left]
                rin[slot, pl.ds(aligned(o * pad + main), 16)] = lift[...].astype(BF16)
                return carry

            lax.fori_loop(0, parts, lift_rows, 0)

        for q in range(CHUNKS):
            inward_self(slot, q).wait()
            for offset in peers:
                inward_arrival(slot, q, offset).wait_recv()
        if over:

            @pl.when(me == keeper)
            def _():
                for q in range(CHUNKS):
                    shared_in_self(slot, q).wait()
                    for z in others:
                        shared_in(slot, q, z).wait_recv()

        start = 0
        for q in range(CHUNKS):
            low, count, held, tall = plan.span(q)
            ends = q == 0
            if not first:
                for offset in peers:
                    outward(q, offset).wait_send()

            def couple(cols):
                result = jnp.dot(
                    weight_buf[start : start + parts * count], rin[slot, :, cols], preferred_element_type=F32
                )
                for h in range(parts):
                    sout[h * pad + low : h * pad + low + count, cols] = result[h * count : (h + 1) * count].astype(BF16)

            tiles(couple)
            outward_self(q).start()
            for offset in peers:
                outward(q, offset).start()
            start += parts * count
            if ends and left:
                if not first:
                    for offset in peers:
                        leftover(1, offset, False).wait_send()

                def couple_left(cols):
                    mixed[:, cols] = jnp.dot(
                        weight_buf[parts * main :], rin[slot, :, cols], preferred_element_type=F32
                    )

                tiles(couple_left)
                for h in range(parts):
                    for t in range(base):
                        fold[t * left : (t + 1) * left] = mixed[
                            h * 16 : h * 16 + left, t * width : (t + 1) * width
                        ]
                    sout_l[h] = fold[...].astype(BF16)
                for offset in peers:
                    leftover(1, offset, False).start()
                rout_l[me] = sout_l[me]
            if over:

                @pl.when(me == keeper)
                def _():
                    if not first:
                        for index, target in enumerate(others):
                            shared_out(q, target, index).wait_send()
                    begin = start - parts * count
                    result = jnp.dot(
                        weight_buf[begin : begin + parts * count], rin_x[slot], preferred_element_type=F32
                    ).astype(BF16)
                    for h in range(parts):
                        sout_x[h * pad + low : h * pad + low + count] = result[h * count : (h + 1) * count]
                    if ends and left:
                        tail = jnp.dot(
                            weight_buf[parts * main :], rin_x[slot], preferred_element_type=F32
                        ).astype(BF16)
                        for h in range(parts):
                            sout_x[h * pad + main : h * pad + pad] = tail[h * 16 : (h + 1) * 16]
                    shared_out_self(q).start()
                    for index, target in enumerate(others):
                        shared_out(q, target, index).start()

        if not final:
            set_forcing(step - 1)
        for q in range(CHUNKS):
            low, count, held, tall = plan.span(q)
            ends = q == 0
            position = (steps - 1 - step) * CHUNKS + q
            source_slot = position % 2
            source_copy(position).wait()
            outward_self(q).wait()
            for offset in peers:
                outward_arrival(q, offset).wait_recv()
            if ends and left:
                for offset in peers:
                    leftover(1, offset, True).wait_recv()

                def spread(b, carry):
                    value = rout_l[b].astype(F32)
                    for t in range(base):
                        lift[:left, t * width : (t + 1) * width] = value[t * left : (t + 1) * left]
                    rout[pl.ds(aligned(b * pad + main), 16)] = lift[...].astype(BF16)
                    return carry

                lax.fori_loop(0, parts, spread, 0)
            if over:

                @pl.when(me == keeper)
                def _():
                    shared_out_self(q).wait()

                @pl.when(me != keeper)
                def _():
                    shared_out(q, keeper, 0).wait_recv()

                def restore(b, carry):
                    spot = pl.ds(pl.multiple_of(b * spare, width), spare)
                    across = (((1,), (1,)), ((), ()))
                    extra_out[b, :tall] = lax.dot_general(
                        rout[pl.ds(aligned(b * pad + low), tall)], fill[spot, :lanes], across,
                        preferred_element_type=F32,
                    ) + lax.dot_general(
                        rout_x[low : low + tall], fill[spot, lanes:], across, preferred_element_type=F32
                    )
                    return carry

                lax.fori_loop(0, parts, restore, 0)

            def update(g, carry):
                c = aligned(low + g * 16)
                local = aligned(g * 16)
                for k in range(16):
                    factor[k * lat : (k + 1) * lat] = source_buf[source_slot, local + k].astype(F32)

                def block(b, edges):
                    tips = edges
                    for r in range(rows):
                        i = b * rows + r
                        if r < base:
                            coupled = rout[
                                pl.ds(aligned(b * pad + c), 16), r * width : (r + 1) * width
                            ].astype(F32)
                            if over:
                                coupled = coupled * ocean[pl.ds(i, 1)]
                        else:
                            coupled = extra_out[b, pl.ds(local, 16), (r - base) * width : (r - base + 1) * width]
                        adjoint = state[i, pl.ds(c, 16)] + factor[pl.ds(i, 16, stride=lat)] * coupled
                        state[i, pl.ds(c, 16)] = adjoint
                        place = lane - 2 * i
                        tips = jnp.where((place == 0) | (place == 1), pltpu.roll(adjoint, 2 * i + 1, 1), tips)
                    return tips

                halo_send[position, pl.ds(local, 16)] = lax.fori_loop(
                    0, parts, block, jnp.zeros((16, width), F32)
                )
                halo(position, g, 0).start()
                halo(position, g, 1).start()
                return carry

            lax.fori_loop(0, tall // 16, update, 0)
            if position + 2 < len(order):
                source_copy(position + 2).start()
            if final:
                if q >= 2:
                    out_copy(q - 2).wait()
            else:
                for offset in peers:
                    inward(slot, q, offset).wait_send()
                if over:

                    @pl.when(me != keeper)
                    def _():
                        shared_in(slot, q, me).wait_send()

            begin = (q % 2) * tallest * lat

            def advect(g, carry):
                c = aligned(low + g * 16)
                local = aligned(g * 16)
                halo(position, g, 0).wait()
                halo(position, g, 1).wait()
                stay, px, nx, py, ny = (coef[k, pl.ds(c, 16)] for k in range(5))
                both = jnp.where(
                    lane % 2 == 1,
                    pltpu.roll(halo_recv[position, 0, pl.ds(local, 16)], width - 2, 1),
                    halo_recv[position, 1, pl.ds(local, 16)],
                )

                def block(b, state_of):
                    southern, adjoint = state_of
                    tips = pltpu.roll(both, (width - 2 * b * rows) % width, 1)
                    for r in range(rows):
                        i = b * rows + r
                        northern = state[i + 1, pl.ds(c, 16)]
                        tip = pltpu.roll(tips, width - 2 * r, 1) if r else tips
                        eastern = jnp.where(lane == width - 1, tip, pltpu.roll(adjoint, width - 1, 1))
                        western = jnp.where(lane == 0, tip, pltpu.roll(adjoint, 1, 1))
                        result = stay * adjoint + px * eastern + nx * western
                        result = result + py * northern + ny * southern
                        if final:
                            stage[pl.ds(begin + local * lat + i, 16, stride=lat)] = result
                        else:
                            emit((result + forcing[pl.ds(i, 1)]) * ocean[pl.ds(i, 1)], i, b, r, c, local)
                        southern, adjoint = adjoint, northern
                    return southern, adjoint

                lax.fori_loop(0, parts, block, (jnp.zeros((16, width), F32), state[0, pl.ds(c, 16)]))
                return carry

            lax.fori_loop(0, tall // 16, advect, 0)
            if final:
                out_copy(q).start()
            else:
                send_inward((step - 1) % 2, q, False)

    for q in range(CHUNKS):
        for offset in peers:
            inward(0, q, offset).wait_send()
            outward(q, offset).wait_send()
        if over:

            @pl.when(me == keeper)
            def _():
                for index, target in enumerate(others):
                    shared_out(q, target, index).wait_send()

            @pl.when(me != keeper)
            def _():
                shared_in(0, q, me).wait_send()

    if left:
        for offset in peers:
            leftover(0, offset, False).wait_send()
            leftover(1, offset, False).wait_send()
    for q in range(max(CHUNKS - 2, 0), CHUNKS):
        out_copy(q).wait()


def call(plan, identity, lam, source, mixing, drift_x, drift_y, ocean_mask, misfit, obs_mask):
    vmem = pl.BlockSpec(memory_space=pltpu.VMEM)
    smem = pl.BlockSpec(memory_space=pltpu.SMEM)
    hbm = pl.BlockSpec(memory_space=pl.ANY)
    dma = pltpu.SemaphoreType.DMA
    parts, pad, lanes, lat, width = plan.parts, plan.pad, plan.lanes, plan.lat, plan.width
    tallest = plan.tallest
    positions = plan.steps * CHUNKS
    spare = max(plan.spare, width)
    filling = (parts * spare, lanes + width) if plan.over else (16, width)
    tile = (pad, width) if plan.over else (16, width)
    gathered = (parts * pad, width) if plan.over else (16, width)
    folded = max(plan.folded, 16)
    left = (parts, folded, width)
    return pl.pallas_call(
        functools.partial(kernel, plan),
        out_shape=jax.ShapeDtypeStruct((plan.own * lat, width), F32),
        in_specs=[hbm, hbm, hbm, smem, smem, vmem, vmem, vmem],
        out_specs=hbm,
        scratch_shapes=[
            pltpu.VMEM((lat + 1, pad, width), F32),
            pltpu.VMEM((parts * pad, lanes), BF16),
            pltpu.VMEM((2, parts * pad, lanes), BF16),
            pltpu.VMEM((parts * pad, lanes), BF16),
            pltpu.VMEM((parts * pad, lanes), BF16),
            pltpu.VMEM(tile, BF16), pltpu.VMEM((2,) + gathered, BF16), pltpu.VMEM(gathered, BF16), pltpu.VMEM(tile, BF16),
            pltpu.VMEM(left, BF16), pltpu.VMEM(left, BF16), pltpu.VMEM(left, BF16), pltpu.VMEM(left, BF16),
            pltpu.VMEM((parts * pad, parts * pad), BF16),
            pltpu.VMEM((round_up(parts * pad, 128), parts * plan.own), BF16),
            pltpu.VMEM((2 * tallest * lat, width), F32),
            pltpu.VMEM((2, tallest, lat, width), BF16),
            pltpu.VMEM((16 * lat, width), F32),
            pltpu.VMEM((5, pad, width), F32),
            pltpu.VMEM((lat, width), F32),
            pltpu.VMEM((lat, width), F32),
            pltpu.VMEM((lat, width), F32),
            pltpu.VMEM((lat, width), F32),
            pltpu.VMEM(filling, BF16),
            pltpu.VMEM((parts, tallest, spare), BF16),
            pltpu.VMEM((parts, tallest, spare), F32),
            pltpu.VMEM((folded, width), F32),
            pltpu.VMEM((parts * 16, lanes), F32),
            pltpu.VMEM((16, lanes), F32),
            pltpu.VMEM((positions, tallest, width), F32),
            pltpu.VMEM((positions, 2, tallest, width), F32),
            dma((2, CHUNKS, parts)),
            dma((2, CHUNKS, parts)),
            dma((2, CHUNKS, parts)),
            dma((2, CHUNKS, parts)),
            dma((2, parts)),
            dma((2, parts)),
            dma((positions, tallest // 16, 2)),
            dma((positions, tallest // 16, 2)),
            dma((2,)),
            dma((2,)),
            dma,
            dma((2, CHUNKS)),
            dma((2, CHUNKS)),
        ],
        compiler_params=pltpu.CompilerParams(
            collective_id=identity, has_side_effects=True, vmem_limit_bytes=62 * 1024 * 1024
        ),
    )(lam, source, mixing, drift_x, drift_y, ocean_mask, misfit, obs_mask)


def census_kernel(ring, plan, ocean_mask, most, mine, others, send_sem, recv_sem):
    lon = lax.axis_index("lon")
    rows = plan.rows
    barrier = pltpu.get_barrier_semaphore()
    for k in range(1, ring):
        pl.semaphore_signal(barrier, inc=1, device_id={"lon": lax.rem(lon + k, ring)}, device_id_type=MESH)
    worst = jnp.zeros((8, 128), F32)
    for b in range(plan.parts):
        count = jnp.sum(ocean_mask[b * rows : (b + 1) * rows].astype(F32))
        worst = worst + jnp.full((8, 128), jnp.maximum(count - plan.lanes, 0.0), F32)
    mine[...] = worst
    pl.semaphore_wait(barrier, ring - 1)

    def copy(k, arriving):
        other = lax.rem(lon + k, ring)
        place = other if arriving else lon
        return pltpu.make_async_remote_copy(
            src_ref=mine,
            dst_ref=others.at[place],
            send_sem=send_sem.at[k],
            recv_sem=recv_sem.at[place],
            device_id={"lon": other},
            device_id_type=MESH,
        )

    for k in range(1, ring):
        copy(k, False).start()
    for k in range(1, ring):
        copy(k, True).wait_recv()
        worst = jnp.maximum(worst, others[lax.rem(lon + k, ring)])
    for k in range(1, ring):
        copy(k, False).wait_send()
    most[0] = jnp.max(worst)


def census(ring, plan, ocean_mask):
    vmem = pl.BlockSpec(memory_space=pltpu.VMEM)
    return pl.pallas_call(
        functools.partial(census_kernel, ring, plan),
        out_shape=jax.ShapeDtypeStruct((1,), F32),
        in_specs=[vmem],
        out_specs=pl.BlockSpec(memory_space=pltpu.SMEM),
        scratch_shapes=[
            pltpu.VMEM((8, 128), F32),
            pltpu.VMEM((ring, 8, 128), F32),
            pltpu.SemaphoreType.DMA((ring,)),
            pltpu.SemaphoreType.DMA((ring,)),
        ],
        compiler_params=pltpu.CompilerParams(collective_id=0, has_side_effects=True),
    )(ocean_mask)


def per_device(
    parts, ring, lam_final, stored_source, mixing, drift_x, drift_y, ocean_mask, misfit, obs_mask
):
    steps = stored_source.shape[0]
    own, lat, width = lam_final.shape
    rows = lat // parts
    packed = Plan(steps, parts, ring, own, lat, width, rows * 3 // 4)
    whole = Plan(steps, parts, ring, own, lat, width, rows)
    most = census(ring, packed, ocean_mask)
    operands = (
        lam_final.reshape(own * lat, width), stored_source, mixing, drift_x, drift_y, ocean_mask, misfit, obs_mask
    )
    result = lax.cond(
        most[0] <= width,
        functools.partial(call, packed, 1),
        functools.partial(call, whole, 2),
        *operands,
    )
    return result.reshape(own, lat, width)


def solution(mesh):
    in_specs = (
        P("spec", None, "lon"),
        P(None, "spec", None, "lon"),
        P(),
        P(),
        P(),
        P(None, "lon"),
        P(None, None, "lon"),
        P(None, None, "lon"),
    )
    out_specs = P("spec", None, "lon")
    return jax.shard_map(
        functools.partial(per_device, mesh.shape["spec"], mesh.shape["lon"]),
        mesh=mesh, in_specs=in_specs, out_specs=out_specs, check_vma=False,
    )
```
